32 devices in a mesh: gx: 2 (over x), gy: 4 (over z), chaos: 4 (over y, core).
Axes of the slice: x: 2, y: 2, z: 4, core: 2. Of those that a mesh axis runs over, the one named last changes fastest.
Arguments:
- field: float32 [68, 8, 32, 128], P('chaos', 'gx', 'gy'), may hold values from -6 to 6
- source: float32 [68, 8, 32, 128], P('chaos', 'gx', 'gy'), may hold values from -6 to 6
- mean_coef: float32 [8, 32, 128], P('gx', 'gy'), may hold values from 1 to 3
- var_coefs: float32 [10, 8, 32, 128], P(None, 'gx', 'gy'), may hold values from -0.6 to 0.6
- galerkin_cols: int32 [10, 68, 3], replicated, may hold values from 0 to 65
- galerkin_vals: float32 [10, 68, 3], replicated, may hold values from -3 to 3
Outputs:
- smoothed: float32 [68, 8, 32, 128], P('chaos', 'gx', 'gy')
- coarse_residual: float32 [68, 4, 16, 64], P('chaos', 'gx', 'gy')
The draws below stay inside these ranges and needn't reach their ends.
All inputs are finite; a program needn't handle non-finite values.
Results may differ from the reference program's by a relative error of at most 0.0001.
Values sent between devices are 32-bit elements; how exact they have to be, the bound alone decides.
No kernel may reach another device: no remote copies, remote signals or barrier semaphores. Data moves between devices by JAX's collectives and lax.ppermute only.
A program may use at most 128 MiB of HBM per device.

```python
import math
import jax
import jax.numpy as jnp
from jax import lax

P_SIZE = 66
VARS = 10
NB = 3
SLOTS = 68
NX = 8
NY = 32
NZ = 128


def touch_ends(values, stream_key, smallest, largest):
    place = [jax.random.randint(jax.random.fold_in(stream_key, axis), (), 0, length) for axis, length in enumerate(values.shape)]
    widest = values.shape.index(max(values.shape))
    beside = place[:widest] + [(place[widest] + 1) % values.shape[widest]] + place[widest + 1:]
    return values.at[tuple(place)].set(smallest).at[tuple(beside)].set(largest)


def block_levels(rng, shape, split, smallest, high):
    def one(dim, blocks):
        steps = jax.random.uniform(jax.random.fold_in(jax.random.fold_in(rng, 6), dim), (blocks,), jnp.float32, smallest / len(split), high / len(split))
        return jnp.repeat(jnp.exp(steps), shape[dim] // blocks).reshape((-1,) + (1,) * (len(shape) - dim - 1))

    factor_of = one(*split[0])
    for cut in split[1:]:
        factor_of = factor_of * one(*cut)
    return factor_of


def gaussian(rng, extent, deviation, bound, shards=(), kind=jnp.bfloat16):
    loudness = block_levels(rng, extent, shards, -0.22, 0.18) if shards else 1.0
    values = jax.random.normal(rng, extent, jnp.float32) * deviation * loudness
    return jnp.minimum(jnp.maximum(values, -bound), bound).astype(kind)


def setup_inputs(seed: int = 0) -> dict:
    arg_keys = jax.random.split(jax.random.key(seed), 7)
    field = gaussian(arg_keys[0], (SLOTS, NX, NY, NZ), 1.0, 6.0, ((0, 4), (1, 2), (2, 4)), jnp.float32)
    source = gaussian(arg_keys[1], (SLOTS, NX, NY, NZ), 1.0, 6.0, ((0, 4), (1, 2), (2, 4)), jnp.float32)
    mean_coef = jnp.clip(jnp.exp(math.log(3.0) - 1.0986123 * jax.random.uniform(arg_keys[2], (NX, NY, NZ), jnp.float32) ** block_levels(arg_keys[2], (NX, NY, NZ), ((0, 2), (1, 4)), -0.2, 0.2)), 1.0, 3.0)
    var_coefs = jnp.clip(jax.random.uniform(arg_keys[3], (VARS, NX, NY, NZ), jnp.float32, -0.6, 0.6) * block_levels(arg_keys[3], (VARS, NX, NY, NZ), ((1, 2), (2, 4)), -0.4, 0.0), -0.6, 0.6)
    galerkin_cols = touch_ends(jax.random.randint(arg_keys[4], (VARS, SLOTS, NB), 0, P_SIZE), jax.random.fold_in(arg_keys[4], 1), 0, P_SIZE - 1).astype(jnp.int32)
    galerkin_vals = gaussian(arg_keys[5], (VARS, SLOTS, NB), 0.5, 3.0, (), jnp.float32)
    return {"field": field, "source": source, "mean_coef": mean_coef, "var_coefs": var_coefs, "galerkin_cols": galerkin_cols, "galerkin_vals": galerkin_vals}


def build_mixing(galerkin_cols, galerkin_vals):
    slots = galerkin_cols.shape[1]
    match = (galerkin_cols[..., None] == jnp.arange(slots, dtype=jnp.int32)).astype(jnp.float32)
    return jnp.sum(match * galerkin_vals[..., None], axis=2)


def laplace(field):
    padded = jnp.pad(field, ((0, 0), (1, 1), (1, 1), (1, 1)))
    beside = padded[:, 2:, 1:-1, 1:-1] + padded[:, :-2, 1:-1, 1:-1]
    beside = beside + padded[:, 1:-1, 2:, 1:-1] + padded[:, 1:-1, :-2, 1:-1]
    beside = beside + padded[:, 1:-1, 1:-1, 2:] + padded[:, 1:-1, 1:-1, :-2]
    return 6.0 * field - beside


def operate(field, mean_coef, var_coefs, mixing):
    lap = laplace(field)
    flat = lap.reshape(lap.shape[0], -1)

    def step(total, inputs):
        matrix, coef = inputs
        mixed = jnp.dot(matrix, flat, precision=lax.Precision.HIGHEST).reshape(lap.shape)
        return total + coef[None] * mixed, None

    coupled, unused = lax.scan(step, jnp.zeros(lap.shape, jnp.float32), (mixing, var_coefs))
    return mean_coef[None] * lap + coupled


def halve(values, axis):
    even = lax.slice_in_dim(values, 0, values.shape[axis], 2, axis)
    odd = lax.slice_in_dim(values, 1, values.shape[axis], 2, axis)
    lower = lax.slice_in_dim(odd, 0, odd.shape[axis] - 1, 1, axis)
    prev = jnp.concatenate([jnp.zeros_like(lax.slice_in_dim(odd, 0, 1, 1, axis)), lower], axis)
    return 0.5 * even + 0.25 * (odd + prev)


def reference(field, source, mean_coef, var_coefs, galerkin_cols, galerkin_vals):
    slots = field.shape[0]
    mask = (jnp.arange(slots, dtype=jnp.int32) < P_SIZE).astype(jnp.float32)[:, None, None, None]
    mixing = build_mixing(galerkin_cols, galerkin_vals)
    start = mask * field
    first = source - operate(start, mean_coef, var_coefs, mixing)
    smoothed = mask * (start + (2.0 / 3.0) * first / (6.0 * mean_coef[None]))
    after = mask * (source - operate(smoothed, mean_coef, var_coefs, mixing))
    coarse = halve(halve(halve(after, 1), 2), 3)
    return smoothed, coarse
```

```python
import functools

import jax
import jax.numpy as jnp
from jax import lax
from jax.experimental import pallas as pl
from jax.experimental.pallas import tpu as pltpu
from jax.sharding import PartitionSpec as P

P_SIZE = 66
VMEM = pl.BlockSpec(memory_space=pltpu.VMEM)
SMEM = pl.BlockSpec(memory_space=pltpu.SMEM)


def partner(i, phase, n):
    j = i + 1 if i % 2 == phase else i - 1
    return j if 0 <= j < n else i


def pair_pairs(phase, n):
    return [(i, partner(i, phase, n)) for i in range(n)]


def phases(n):
    return 1 if n == 2 else 2


def swap_sides(low, high, axis):
    n = lax.axis_size(axis)
    even = lax.axis_index(axis) % 2 == 0
    picks = [jnp.where(even, high, low), jnp.where(even, low, high)]
    return [lax.ppermute(picks[p], axis, pair_pairs(p, n)) for p in range(phases(n))]


def side_flags(axis):
    n = lax.axis_size(axis)
    i = lax.axis_index(axis)
    odd = lax.rem(i, 2)
    flags = []
    for p in range(phases(n)):
        up = jnp.logical_and(odd == p, i + 1 < n)
        down = jnp.logical_and(odd != p, i > 0)
        flags.append((jnp.where(down, 1.0, 0.0), jnp.where(up, 1.0, 0.0)))
    return flags


def lap_kernel(nx, ny, u_ref, *refs):
    xs, ys, out_ref = refs[:nx], refs[nx:nx + ny], refs[nx + ny]
    n, X, Y, Z = u_ref.shape
    fx, fy = side_flags("gx"), side_flags("gy")
    sub = lax.broadcasted_iota(jnp.int32, (Y, Z), 0)
    lane = lax.broadcasted_iota(jnp.int32, (Y, Z), 1)
    for s in range(n):
        plane = [u_ref[s, x] for x in range(X)]
        below = sum(f[0] * r[s] for f, r in zip(fx, xs))
        above = sum(f[1] * r[s] for f, r in zip(fx, xs))
        row_lo = sum(f[0] * r[s] for f, r in zip(fy, ys))
        row_hi = sum(f[1] * r[s] for f, r in zip(fy, ys))
        for x in range(X):
            v = plane[x]
            near = (plane[x - 1] if x else below) + (plane[x + 1] if x + 1 < X else above)
            near += jnp.where(sub == 0, row_lo[x:x + 1], pltpu.roll(v, 1, 0))
            near += jnp.where(sub == Y - 1, row_hi[x:x + 1], pltpu.roll(v, Y - 1, 0))
            near += jnp.where(lane == 0, 0.0, pltpu.roll(v, 1, 1))
            near += jnp.where(lane == Z - 1, 0.0, pltpu.roll(v, Z - 1, 1))
            out_ref[s, x] = 6.0 * v - near


def laplace(u, xs, ys):
    return pl.pallas_call(
        functools.partial(lap_kernel, len(xs), len(ys)),
        out_shape=jax.ShapeDtypeStruct(u.shape, u.dtype),
        in_specs=[VMEM] * (1 + len(xs) + len(ys)),
        out_specs=VMEM,
        name="laplace",
    )(u, *xs, *ys)


def gather_blocks(own):
    n = lax.axis_size("chaos")
    blocks = {0: own}
    d = n // 2
    while d:
        for p in list(blocks):
            blocks[p ^ d] = lax.ppermute(blocks[p], "chaos", [(i, i ^ d) for i in range(n)])
        d //= 2
    return [blocks[p] for p in range(n)]


def fill_slots(me, blocks, full_ref):
    n = blocks[0].shape[0]
    for p, ref in enumerate(blocks):
        base = (me ^ p) * n
        for s in range(n):
            full_ref[base + s] = ref[s]


def mixed_row(i, n, cols_ref, vals_ref, full_ref, var_ref):
    K = var_ref.shape[0]
    nb = cols_ref.shape[0] // (K * n)
    acc = None
    for k in range(K):
        m = None
        for b in range(nb):
            at = (k * n + i) * nb + b
            t = vals_ref[at] * full_ref[cols_ref[at]]
            m = t if m is None else m + t
        m = var_ref[k] * m
        acc = m if acc is None else acc + m
    return acc


def sweep_kernel(nb, nx, ny, cols_ref, vals_ref, var_ref, mean_ref, source_ref, u_ref, *refs):
    blocks, refs = refs[:nb], refs[nb:]
    out_ref, refs = refs[0], refs[1:]
    xs, ys, full_ref = refs[:nx], refs[nx:nx + ny], refs[nx + ny]
    n, X, Y, Z = u_ref.shape
    me = lax.axis_index("chaos")
    fill_slots(me, blocks, full_ref)
    mean = mean_ref[...]
    inv = 1.0 / (9.0 * mean)

    def row(i, carry):
        acc = mixed_row(i, n, cols_ref, vals_ref, full_ref, var_ref)
        first = source_ref[i] - (mean * blocks[0][i] + acc)
        keep = jnp.where(me * n + i < P_SIZE, 1.0, 0.0)
        out_ref[i] = keep * (u_ref[i] + first * inv)
        return carry

    lax.fori_loop(0, n, row, 0)
    x_even = lax.rem(lax.axis_index("gx"), 2) == 0
    y_even = lax.rem(lax.axis_index("gy"), 2) == 0
    for p, ref in enumerate(xs):
        at = jnp.where(x_even if p == 0 else jnp.logical_not(x_even), X - 1, 0)
        for s in range(n):
            ref[s] = out_ref[s, at]
    low, high = out_ref[:, :, 0, :], out_ref[:, :, Y - 1, :]
    flag = jnp.where(y_even, 1.0, 0.0)
    for p, ref in enumerate(ys):
        f = flag if p == 0 else 1.0 - flag
        ref[...] = f * high + (1.0 - f) * low


def sweep(cols, vals, var, mean, source, u, blocks, nx, ny):
    n, X, Y, Z = u.shape
    total = n * len(blocks)
    outs = [jax.ShapeDtypeStruct(u.shape, u.dtype)]
    outs += [jax.ShapeDtypeStruct((n, Y, Z), u.dtype)] * nx
    outs += [jax.ShapeDtypeStruct((n, X, Z), u.dtype)] * ny
    res = pl.pallas_call(
        functools.partial(sweep_kernel, len(blocks), nx, ny),
        out_shape=outs,
        in_specs=[SMEM, SMEM] + [VMEM] * (4 + len(blocks)),
        out_specs=[VMEM] * len(outs),
        scratch_shapes=[pltpu.VMEM((total, X, Y, Z), u.dtype)],
        name="sweep",
    )(cols, vals, var, mean, source, u, *blocks)
    return res[0], res[1:1 + nx], res[1 + nx:]


def residual_kernel(nb, cols_ref, vals_ref, var_ref, mean_ref, source_ref, *refs):
    blocks = refs[:nb]
    part_ref, edge_ref, full_ref, x_ref, z_ref = refs[nb:]
    n, X, Y, Z = source_ref.shape
    me = lax.axis_index("chaos")
    fill_slots(me, blocks, full_ref)
    mean = mean_ref[...]
    A = X // 2 + 1

    def row(i, carry):
        acc = mixed_row(i, n, cols_ref, vals_ref, full_ref, var_ref)
        keep = jnp.where(me * n + i < P_SIZE, 1.0, 0.0)
        after = keep * (source_ref[i] - (mean * blocks[0][i] + acc))
        at = pl.multiple_of(i * (A * Y), A * Y)
        for a in range(A):
            t = 0.25 * after[2 * a - 1] if a else None
            if 2 * a < X:
                more = 0.5 * after[2 * a] + 0.25 * after[2 * a + 1]
                t = more if t is None else t + more
            x_ref[pl.ds(at + a * Y, Y), :] = t
        return carry

    lax.fori_loop(0, n, row, 0)
    c = lax.broadcasted_iota(jnp.int32, (Z, Z // 2), 1) * 2
    z = lax.broadcasted_iota(jnp.int32, (Z, Z // 2), 0)
    weight = jnp.where(z == c, 0.5, jnp.where(jnp.abs(z - c) == 1, 0.25, 0.0)).astype(jnp.float32)
    z_ref[...] = jnp.dot(x_ref[...], weight, precision=lax.Precision.HIGHEST, preferred_element_type=jnp.float32)
    rows = n * A * Y
    even = z_ref[pl.ds(0, rows // 2, stride=2), :].reshape(n * A, Y // 2, Z // 2)
    odd = z_ref[pl.ds(1, rows // 2, stride=2), :].reshape(n * A, Y // 2, Z // 2)
    sub = lax.broadcasted_iota(jnp.int32, (n * A, Y // 2, Z // 2), 1)
    prev = jnp.where(sub == 0, 0.0, jnp.concatenate([odd[:, :1], odd[:, :-1]], 1))
    part_ref[...] = (0.5 * even + 0.25 * (odd + prev)).reshape(part_ref.shape)
    edge_ref[...] = (0.25 * odd[:, Y // 2 - 1]).reshape(edge_ref.shape)


def residual(cols, vals, var, mean, source, blocks):
    n, X, Y, Z = source.shape
    total = n * len(blocks)
    A = X // 2 + 1
    return pl.pallas_call(
        functools.partial(residual_kernel, len(blocks)),
        out_shape=[jax.ShapeDtypeStruct((n, A, Y // 2, Z // 2), source.dtype),
                   jax.ShapeDtypeStruct((n, A, Z // 2), source.dtype)],
        in_specs=[SMEM, SMEM] + [VMEM] * (3 + len(blocks)),
        out_specs=[VMEM] * 2,
        scratch_shapes=[pltpu.VMEM((total, X, Y, Z), source.dtype),
                        pltpu.VMEM((n * A * Y, Z), source.dtype),
                        pltpu.VMEM((n * A * Y, Z // 2), source.dtype)],
        name="residual",
    )(cols, vals, var, mean, source, *blocks)


def body(field, source, mean_coef, var_coefs, galerkin_cols, galerkin_vals):
    n, X, Y, Z = field.shape
    first_row = lax.axis_index("chaos") * n
    cols = lax.dynamic_slice_in_dim(galerkin_cols, first_row, n, 1).reshape(-1)
    vals = lax.dynamic_slice_in_dim(galerkin_vals, first_row, n, 1).reshape(-1)
    gx, gy = lax.axis_size("gx"), lax.axis_size("gy")

    xs = swap_sides(field[:, 0], field[:, X - 1], "gx")
    ys = swap_sides(field[:, :, 0], field[:, :, Y - 1], "gy")
    blocks = gather_blocks(laplace(field, xs, ys))
    smoothed, xs, ys = sweep(cols, vals, var_coefs, mean_coef, source, field, blocks, phases(gx), phases(gy))

    xs = [lax.ppermute(v, "gx", pair_pairs(p, gx)) for p, v in enumerate(xs)]
    ys = [lax.ppermute(v, "gy", pair_pairs(p, gy)) for p, v in enumerate(ys)]
    blocks = gather_blocks(laplace(smoothed, xs, ys))
    part, edge = residual(cols, vals, var_coefs, mean_coef, source, blocks)

    up_x = [(i, i + 1) for i in range(gx - 1)]
    up_y = [(i, i + 1) for i in range(gy - 1)]
    up_xy = [(i * gy + j, (i + 1) * gy + j + 1) for i in range(gx - 1) for j in range(gy - 1)]
    A = X // 2
    from_x = lax.ppermute(part[:, A], "gx", up_x)
    from_y = lax.ppermute(edge[:, :A], "gy", up_y)
    from_xy = lax.ppermute(edge[:, A], ("gx", "gy"), up_xy)
    from_y = jnp.concatenate([from_y[:, :1] + from_xy[:, None], from_y[:, 1:]], 1)
    coarse = part[:, :A]
    coarse = jnp.concatenate([coarse[:, :1] + from_x[:, None], coarse[:, 1:]], 1)
    coarse = jnp.concatenate([coarse[:, :, :1] + from_y[:, :, None], coarse[:, :, 1:]], 2)
    return smoothed, coarse


def solution(mesh):
    return jax.shard_map(
        body,
        mesh=mesh,
        in_specs=(
            P("chaos", "gx", "gy", None),
            P("chaos", "gx", "gy", None),
            P("gx", "gy", None),
            P(None, "gx", "gy", None),
            P(),
            P(),
        ),
        out_specs=(P("chaos", "gx", "gy", None), P("chaos", "gx", "gy", None)),
        check_vma=False,
    )
```

```python
import functools

import jax
import jax.numpy as jnp
from jax import lax
from jax.experimental import pallas as pl
from jax.experimental.pallas import tpu as pltpu
from jax.sharding import PartitionSpec as P

P_SIZE = 66
PARAMS = pltpu.CompilerParams(vmem_limit_bytes=12 << 20)
VMEM = pl.BlockSpec(memory_space=pltpu.VMEM)
SMEM = pl.BlockSpec(memory_space=pltpu.SMEM)


def partner(i, phase, n):
    j = i + 1 if i % 2 == phase else i - 1
    return j if 0 <= j < n else i


def pair_pairs(phase, n):
    return [(i, partner(i, phase, n)) for i in range(n)]


def phases(n):
    return 1 if n == 2 else 2


def swap_sides(low, high, axis):
    n = lax.axis_size(axis)
    even = lax.axis_index(axis) % 2 == 0
    picks = [jnp.where(even, high, low), jnp.where(even, low, high)]
    return [lax.ppermute(picks[p], axis, pair_pairs(p, n)) for p in range(phases(n))]


def side_flags(axis):
    n = lax.axis_size(axis)
    i = lax.axis_index(axis)
    odd = lax.rem(i, 2)
    flags = []
    for p in range(phases(n)):
        up = jnp.logical_and(odd == p, i + 1 < n)
        down = jnp.logical_and(odd != p, i > 0)
        flags.append((jnp.where(down, 1.0, 0.0), jnp.where(up, 1.0, 0.0)))
    return flags


def lap_kernel(nx, ny, u_ref, *refs):
    xs, ys, out_ref = refs[:nx], refs[nx:nx + ny], refs[nx + ny]
    n, X, Y, Z = u_ref.shape
    fx, fy = side_flags("gx"), side_flags("gy")
    sub = lax.broadcasted_iota(jnp.int32, (Y, Z), 0)
    lane = lax.broadcasted_iota(jnp.int32, (Y, Z), 1)
    for s in range(n):
        plane = [u_ref[s, x] for x in range(X)]
        below = sum(f[0] * r[s] for f, r in zip(fx, xs))
        above = sum(f[1] * r[s] for f, r in zip(fx, xs))
        row_lo = sum(f[0] * r[s] for f, r in zip(fy, ys))
        row_hi = sum(f[1] * r[s] for f, r in zip(fy, ys))
        for x in range(X):
            v = plane[x]
            near = (plane[x - 1] if x else below) + (plane[x + 1] if x + 1 < X else above)
            near += jnp.where(sub == 0, row_lo[x:x + 1], pltpu.roll(v, 1, 0))
            near += jnp.where(sub == Y - 1, row_hi[x:x + 1], pltpu.roll(v, Y - 1, 0))
            near += jnp.where(lane == 0, 0.0, pltpu.roll(v, 1, 1))
            near += jnp.where(lane == Z - 1, 0.0, pltpu.roll(v, Z - 1, 1))
            out_ref[s, x] = 6.0 * v - near


def laplace(u, xs, ys):
    return pl.pallas_call(
        functools.partial(lap_kernel, len(xs), len(ys)),
        out_shape=jax.ShapeDtypeStruct(u.shape, u.dtype),
        in_specs=[VMEM] * (1 + len(xs) + len(ys)),
        out_specs=VMEM,
        compiler_params=PARAMS,
        name="laplace",
    )(u, *xs, *ys)


def gather_blocks(own):
    n = lax.axis_size("chaos")
    blocks = {0: own}
    d = n // 2
    while d:
        for p in list(blocks):
            blocks[p ^ d] = lax.ppermute(blocks[p], "chaos", [(i, i ^ d) for i in range(n)])
        d //= 2
    return [blocks[p] for p in range(n)]


def fill_slots(me, blocks, full_ref):
    n = blocks[0].shape[0]
    for p, ref in enumerate(blocks):
        base = (me ^ p) * n
        for s in range(n):
            full_ref[base + s] = ref[s]


def mixed_row(i, n, cols_ref, vals_ref, full_ref, var_ref):
    K = var_ref.shape[0]
    nb = cols_ref.shape[0] // (K * n)
    acc = None
    for k in range(K):
        m = None
        for b in range(nb):
            at = (k * n + i) * nb + b
            t = vals_ref[at] * full_ref[cols_ref[at]]
            m = t if m is None else m + t
        m = var_ref[k] * m
        acc = m if acc is None else acc + m
    return acc


def sweep_kernel(nb, nx, ny, cols_ref, vals_ref, var_ref, mean_ref, source_ref, u_ref, *refs):
    blocks, refs = refs[:nb], refs[nb:]
    out_ref, refs = refs[0], refs[1:]
    xs, ys, full_ref = refs[:nx], refs[nx:nx + ny], refs[nx + ny]
    n, X, Y, Z = u_ref.shape
    me = lax.axis_index("chaos")
    fill_slots(me, blocks, full_ref)
    mean = mean_ref[...]
    inv = 1.0 / (9.0 * mean)

    def row(i, carry):
        acc = mixed_row(i, n, cols_ref, vals_ref, full_ref, var_ref)
        first = source_ref[i] - (mean * blocks[0][i] + acc)
        keep = jnp.where(me * n + i < P_SIZE, 1.0, 0.0)
        out_ref[i] = keep * (u_ref[i] + first * inv)
        return carry

    lax.fori_loop(0, n, row, 0)
    x_even = lax.rem(lax.axis_index("gx"), 2) == 0
    y_even = lax.rem(lax.axis_index("gy"), 2) == 0
    for p, ref in enumerate(xs):
        at = jnp.where(x_even if p == 0 else jnp.logical_not(x_even), X - 1, 0)
        for s in range(n):
            ref[s] = out_ref[s, at]
    low, high = out_ref[:, :, 0, :], out_ref[:, :, Y - 1, :]
    flag = jnp.where(y_even, 1.0, 0.0)
    for p, ref in enumerate(ys):
        f = flag if p == 0 else 1.0 - flag
        ref[...] = f * high + (1.0 - f) * low


def sweep(cols, vals, var, mean, source, u, blocks, nx, ny):
    n, X, Y, Z = u.shape
    total = n * len(blocks)
    outs = [jax.ShapeDtypeStruct(u.shape, u.dtype)]
    outs += [jax.ShapeDtypeStruct((n, Y, Z), u.dtype)] * nx
    outs += [jax.ShapeDtypeStruct((n, X, Z), u.dtype)] * ny
    res = pl.pallas_call(
        functools.partial(sweep_kernel, len(blocks), nx, ny),
        out_shape=outs,
        in_specs=[SMEM, SMEM] + [VMEM] * (4 + len(blocks)),
        out_specs=[VMEM] * len(outs),
        scratch_shapes=[pltpu.VMEM((total, X, Y, Z), u.dtype)],
        compiler_params=PARAMS,
        name="sweep",
    )(cols, vals, var, mean, source, u, *blocks)
    return res[0], res[1:1 + nx], res[1 + nx:]


def residual_kernel(nb, cols_ref, vals_ref, var_ref, mean_ref, source_ref, *refs):
    blocks = refs[:nb]
    part_ref, edge_ref, full_ref, x_ref, z_ref = refs[nb:]
    n, X, Y, Z = source_ref.shape
    me = lax.axis_index("chaos")
    fill_slots(me, blocks, full_ref)
    mean = mean_ref[...]
    A = X // 2 + 1

    def row(i, carry):
        acc = mixed_row(i, n, cols_ref, vals_ref, full_ref, var_ref)
        keep = jnp.where(me * n + i < P_SIZE, 1.0, 0.0)
        after = keep * (source_ref[i] - (mean * blocks[0][i] + acc))
        at = pl.multiple_of(i * (A * Y), A * Y)
        for a in range(A):
            t = 0.25 * after[2 * a - 1] if a else None
            if 2 * a < X:
                more = 0.5 * after[2 * a] + 0.25 * after[2 * a + 1]
                t = more if t is None else t + more
            x_ref[pl.ds(at + a * Y, Y), :] = t
        return carry

    lax.fori_loop(0, n, row, 0)
    c = lax.broadcasted_iota(jnp.int32, (Z, Z // 2), 1) * 2
    z = lax.broadcasted_iota(jnp.int32, (Z, Z // 2), 0)
    weight = jnp.where(z == c, 0.5, jnp.where(jnp.abs(z - c) == 1, 0.25, 0.0)).astype(jnp.float32)
    z_ref[...] = jnp.dot(x_ref[...], weight, precision=lax.Precision.HIGHEST, preferred_element_type=jnp.float32)
    rows = n * A * Y
    even = z_ref[pl.ds(0, rows // 2, stride=2), :].reshape(n * A, Y // 2, Z // 2)
    odd = z_ref[pl.ds(1, rows // 2, stride=2), :].reshape(n * A, Y // 2, Z // 2)
    sub = lax.broadcasted_iota(jnp.int32, (n * A, Y // 2, Z // 2), 1)
    prev = jnp.where(sub == 0, 0.0, jnp.concatenate([odd[:, :1], odd[:, :-1]], 1))
    part_ref[...] = (0.5 * even + 0.25 * (odd + prev)).reshape(part_ref.shape)
    edge_ref[...] = (0.25 * odd[:, Y // 2 - 1]).reshape(edge_ref.shape)


def residual(cols, vals, var, mean, source, blocks):
    n, X, Y, Z = source.shape
    total = n * len(blocks)
    A = X // 2 + 1
    return pl.pallas_call(
        functools.partial(residual_kernel, len(blocks)),
        out_shape=[jax.ShapeDtypeStruct((n, A, Y // 2, Z // 2), source.dtype),
                   jax.ShapeDtypeStruct((n, A, Z // 2), source.dtype)],
        in_specs=[SMEM, SMEM] + [VMEM] * (3 + len(blocks)),
        out_specs=[VMEM] * 2,
        scratch_shapes=[pltpu.VMEM((total, X, Y, Z), source.dtype),
                        pltpu.VMEM((n * A * Y, Z), source.dtype),
                        pltpu.VMEM((n * A * Y, Z // 2), source.dtype)],
        compiler_params=PARAMS,
        name="residual",
    )(cols, vals, var, mean, source, *blocks)


def body(field, source, mean_coef, var_coefs, galerkin_cols, galerkin_vals):
    n, X, Y, Z = field.shape
    first_row = lax.axis_index("chaos") * n
    cols = lax.dynamic_slice_in_dim(galerkin_cols, first_row, n, 1).reshape(-1)
    vals = lax.dynamic_slice_in_dim(galerkin_vals, first_row, n, 1).reshape(-1)
    gx, gy = lax.axis_size("gx"), lax.axis_size("gy")

    xs = swap_sides(field[:, 0], field[:, X - 1], "gx")
    ys = swap_sides(field[:, :, 0], field[:, :, Y - 1], "gy")
    blocks = gather_blocks(laplace(field, xs, ys))
    smoothed, xs, ys = sweep(cols, vals, var_coefs, mean_coef, source, field, blocks, phases(gx), phases(gy))

    xs = [lax.ppermute(v, "gx", pair_pairs(p, gx)) for p, v in enumerate(xs)]
    ys = [lax.ppermute(v, "gy", pair_pairs(p, gy)) for p, v in enumerate(ys)]
    blocks = gather_blocks(laplace(smoothed, xs, ys))
    part, edge = residual(cols, vals, var_coefs, mean_coef, source, blocks)

    up_x = [(i, i + 1) for i in range(gx - 1)]
    up_y = [(i, i + 1) for i in range(gy - 1)]
    up_xy = [(i * gy + j, (i + 1) * gy + j + 1) for i in range(gx - 1) for j in range(gy - 1)]
    A = X // 2
    from_x = lax.ppermute(part[:, A], "gx", up_x)
    from_y = lax.ppermute(edge[:, :A], "gy", up_y)
    from_xy = lax.ppermute(edge[:, A], ("gx", "gy"), up_xy)
    from_y = jnp.concatenate([from_y[:, :1] + from_xy[:, None], from_y[:, 1:]], 1)
    coarse = part[:, :A]
    coarse = jnp.concatenate([coarse[:, :1] + from_x[:, None], coarse[:, 1:]], 1)
    coarse = jnp.concatenate([coarse[:, :, :1] + from_y[:, :, None], coarse[:, :, 1:]], 2)
    return smoothed, coarse


def solution(mesh):
    return jax.shard_map(
        body,
        mesh=mesh,
        in_specs=(
            P("chaos", "gx", "gy", None),
            P("chaos", "gx", "gy", None),
            P("gx", "gy", None),
            P(None, "gx", "gy", None),
            P(),
            P(),
        ),
        out_specs=(P("chaos", "gx", "gy", None), P("chaos", "gx", "gy", None)),
        check_vma=False,
    )
```

```python
import functools

import jax
import jax.numpy as jnp
from jax import lax
from jax.experimental import pallas as pl
from jax.experimental.pallas import tpu as pltpu
from jax.sharding import PartitionSpec as P

P_SIZE = 66
PARAMS = pltpu.CompilerParams(vmem_limit_bytes=12 << 20)
VMEM = pl.BlockSpec(memory_space=pltpu.VMEM)
SMEM = pl.BlockSpec(memory_space=pltpu.SMEM)


def partner(i, phase, n):
    j = i + 1 if i % 2 == phase else i - 1
    return j if 0 <= j < n else i


def pair_pairs(phase, n):
    return [(i, partner(i, phase, n)) for i in range(n)]


def phases(n):
    return 1 if n == 2 else 2


def swap_sides(low, high, axis):
    n = lax.axis_size(axis)
    even = lax.axis_index(axis) % 2 == 0
    picks = [jnp.where(even, high, low), jnp.where(even, low, high)]
    return [lax.ppermute(picks[p], axis, pair_pairs(p, n)) for p in range(phases(n))]


def side_flags(axis):
    n = lax.axis_size(axis)
    i = lax.axis_index(axis)
    odd = lax.rem(i, 2)
    flags = []
    for p in range(phases(n)):
        up = jnp.logical_and(odd == p, i + 1 < n)
        down = jnp.logical_and(odd != p, i > 0)
        flags.append((jnp.where(down, 1.0, 0.0), jnp.where(up, 1.0, 0.0)))
    return flags


def lap_kernel(nx, ny, u_ref, *refs):
    xs, ys, out_ref = refs[:nx], refs[nx:nx + ny], refs[nx + ny]
    n, X, Y, Z = u_ref.shape
    fx, fy = side_flags("gx"), side_flags("gy")
    sub = lax.broadcasted_iota(jnp.int32, (Y, Z), 0)
    lane = lax.broadcasted_iota(jnp.int32, (Y, Z), 1)
    for s in range(n):
        plane = [u_ref[s, x] for x in range(X)]
        below = sum(f[0] * r[s] for f, r in zip(fx, xs))
        above = sum(f[1] * r[s] for f, r in zip(fx, xs))
        row_lo = sum(f[0] * r[s] for f, r in zip(fy, ys))
        row_hi = sum(f[1] * r[s] for f, r in zip(fy, ys))
        for x in range(X):
            v = plane[x]
            near = (plane[x - 1] if x else below) + (plane[x + 1] if x + 1 < X else above)
            near += jnp.where(sub == 0, row_lo[x:x + 1], pltpu.roll(v, 1, 0))
            near += jnp.where(sub == Y - 1, row_hi[x:x + 1], pltpu.roll(v, Y - 1, 0))
            near += jnp.where(lane == 0, 0.0, pltpu.roll(v, 1, 1))
            near += jnp.where(lane == Z - 1, 0.0, pltpu.roll(v, Z - 1, 1))
            out_ref[s, x] = 6.0 * v - near


def laplace(u, xs, ys):
    return pl.pallas_call(
        functools.partial(lap_kernel, len(xs), len(ys)),
        out_shape=jax.ShapeDtypeStruct(u.shape, u.dtype),
        in_specs=[VMEM] * (1 + len(xs) + len(ys)),
        out_specs=VMEM,
        compiler_params=PARAMS,
        name="laplace",
    )(u, *xs, *ys)


def gather_blocks(own):
    n = lax.axis_size("chaos")
    blocks = {0: own}
    d = n // 2
    while d:
        for p in list(blocks):
            blocks[p ^ d] = lax.ppermute(blocks[p], "chaos", [(i, i ^ d) for i in range(n)])
        d //= 2
    return [blocks[p] for p in range(n)]


def fill_slots(me, blocks, full_ref):
    n = blocks[0].shape[0]
    for p, ref in enumerate(blocks):
        base = (me ^ p) * n
        for s in range(n):
            full_ref[base + s] = ref[s]


def mixed_row(i, n, cols_ref, vals_ref, full_ref, var_ref):
    K = var_ref.shape[0]
    nb = cols_ref.shape[0] // (K * n)
    acc = None
    for k in range(K):
        m = None
        for b in range(nb):
            at = (k * n + i) * nb + b
            t = vals_ref[at] * full_ref[cols_ref[at]]
            m = t if m is None else m + t
        m = var_ref[k] * m
        acc = m if acc is None else acc + m
    return acc


def row_list(X, Y):
    at = {(x, y): x * Y + y for x in range(X) for y in range(Y)}
    base = X * Y
    at.update({(-1, y): base + y for y in range(Y)})
    at.update({(X, y): base + Y + y for y in range(Y)})
    at.update({(x, -1): base + 2 * Y + x for x in range(X)})
    at.update({(x, Y): base + 2 * Y + X + x for x in range(X)})
    return at


def coarse_sums(X, Y, term):
    cols = {}
    for x in range(-1, X + 1):
        ys = [y for y in range(-1, Y + 1) if 0 <= x < X or 0 <= y < Y]
        got = {y: term(x, y) for y in ys}
        for b in range(-1, Y // 2 + 1):
            taps = [got[y] for y in (2 * b - 1, 2 * b, 2 * b + 1) if got.get(y) is not None]
            if taps:
                cols[x, b] = functools.reduce(jnp.add, taps)
    out = {}
    for a in range(-1, X // 2 + 1):
        for b in range(-1, Y // 2 + 1):
            taps = [cols[x, b] for x in (2 * a - 1, 2 * a, 2 * a + 1) if (x, b) in cols]
            out[a, b] = functools.reduce(jnp.add, taps) if taps else None
    return out


def whole_groups(n):
    return n // 16 * 16


def prep_kernel(P, nx, ny, cols_ref, vals_ref, var_ref, mean_ref, source_ref, *refs):
    xs, ys = refs[:nx], refs[nx:nx + ny]
    v_ref, vt_ref, g_ref, rs_ref, gt_ref = refs[nx + ny + 1:]
    n, X, Y, Z = source_ref.shape
    K = var_ref.shape[0]
    J = whole_groups(n)
    me = lax.axis_index("chaos")
    wide = cols_ref.shape[2]

    fx, fy = side_flags("gx"), side_flags("gy")
    sub = lax.broadcasted_iota(jnp.int32, (Y, Z), 0)
    wy = jnp.where(lax.rem(sub, 2) == 0, 0.5, 0.25)
    base = X * Y
    for k in range(K + 1):
        for x in range(X):
            plane = var_ref[k, x] if k < K else mean_ref[x]
            v_ref[k, x * Y:(x + 1) * Y, :] = plane * (-(0.5 if x % 2 == 0 else 0.25) * wy)
        low = sum(f[0] * r[k] for f, r in zip(fx, xs))
        high = sum(f[1] * r[k] for f, r in zip(fx, xs))
        v_ref[k, base:base + Y, :] = low * (0.25 * wy)
        v_ref[k, base + Y:base + 2 * Y, :] = high * (0.5 * wy)
        low = sum(f[0] * r[k] for f, r in zip(fy, ys))
        high = sum(f[1] * r[k] for f, r in zip(fy, ys))
        wx = jnp.where(lax.rem(lax.broadcasted_iota(jnp.int32, (X, Z), 0), 2) == 0, 0.5, 0.25)
        v_ref[k, base + 2 * Y:base + 2 * Y + X, :] = low * (0.25 * wx)
        v_ref[k, base + 2 * Y + X:base + 2 * Y + 2 * X, :] = high * (0.5 * wx)
    rows = base + 2 * Y + 2 * X
    vt_ref[...] = jnp.zeros_like(vt_ref)
    for k in range(K + 1):
        for e in range(rows // 8):
            vt_ref[8 * e:8 * e + 8, k, :] = v_ref[k, 8 * e:8 * e + 8, :]

    gt_ref[...] = jnp.zeros_like(gt_ref)
    first = me * n
    slot = lax.broadcasted_iota(jnp.int32, (J, wide), 0) + first
    lane = lax.broadcasted_iota(jnp.int32, (J, wide), 1)
    for k in range(K + 1):
        if k < K:
            c, v = cols_ref[k], vals_ref[k]
            v = jnp.where(lax.broadcasted_iota(jnp.int32, v.shape, 1) < P_SIZE, v, 0.0)
            hits = sum(jnp.where(c[b:b + 1] == slot, v[b:b + 1], 0.0) for b in range(c.shape[0]))
            rest = [sum(jnp.where(c[b:b + 1] == first + j, v[b:b + 1], 0.0) for b in range(c.shape[0]))
                    for j in range(J, n)]
        else:
            hits = jnp.where(lane == slot, 1.0, 0.0)
            rest = [jnp.where(lane[:1] == first + j, 1.0, 0.0) for j in range(J, n)]
        gt_ref[k * J:(k + 1) * J, 0:wide] = hits
        for j, r in enumerate(rest):
            at = (K + 1) * J + 16 * j + k
            gt_ref[at:at + 1, 0:wide] = r
    gt = gt_ref[...]
    lanes = lax.broadcasted_iota(jnp.int32, gt.shape, 1)
    total = gt.shape[1]
    step = (n + 7) // 8 * 8
    picked = jnp.zeros_like(gt)
    for p in range(P):
        shift = lax.rem(p * step - (me ^ p) * n + 8 * total, total)
        moved = pltpu.roll(gt, shift, 1)
        picked = jnp.where(jnp.logical_and(lanes >= p * step, lanes < p * step + n), moved, picked)
    g = jnp.transpose(picked)[:P * step]
    depth = g_ref.shape[1]
    hi = g.astype(jnp.bfloat16)
    lo = (g - hi.astype(jnp.float32)).astype(jnp.bfloat16)
    g_ref[0:P * step, :] = hi[:, :depth]
    g_ref[P * step:2 * P * step, :] = lo[:, :depth]

    flat = source_ref.reshape(n * X * Y, Z)
    keep = jnp.where(lax.broadcasted_iota(jnp.int32, (n, Z), 0) + first < P_SIZE, 1.0, 0.0)

    def term(x, y):
        if not (0 <= x < X and 0 <= y < Y):
            return None
        w = (0.5 if x % 2 == 0 else 0.25) * (0.5 if y % 2 == 0 else 0.25)
        return flat[pl.ds(x * Y + y, n, stride=X * Y), :] * (w * keep)

    rs_ref[...] = jnp.zeros_like(rs_ref)
    B = Y // 2 + 2
    for (a, b), t in coarse_sums(X, Y, term).items():
        if t is not None:
            at = ((a + 1) * B + b + 1) * Z
            rs_ref[0:n, at:at + Z] = t


def prep(P, cols, vals, var, mean, source, xs, ys, after):
    n, X, Y, Z = source.shape
    K = var.shape[0]
    rows = X * Y + 2 * Y + 2 * X
    depth = (K + 1) * whole_groups(n) + 16 * (n - whole_groups(n))
    step = (n + 7) // 8 * 8
    wide = (X // 2 + 2) * (Y // 2 + 2) * Z
    return pl.pallas_call(
        functools.partial(prep_kernel, P, len(xs), len(ys)),
        out_shape=[jax.ShapeDtypeStruct((K + 1, rows, Z), jnp.float32),
                   jax.ShapeDtypeStruct((rows, 16, Z), jnp.float32),
                   jax.ShapeDtypeStruct((2 * P * step, depth), jnp.bfloat16),
                   jax.ShapeDtypeStruct((step, wide), jnp.float32)],
        in_specs=[VMEM] * (6 + len(xs) + len(ys)),
        out_specs=[VMEM] * 4,
        scratch_shapes=[pltpu.VMEM(((depth + 127) // 128 * 128, (P * step + 127) // 128 * 128), jnp.float32)],
        compiler_params=PARAMS,
        name="prep",
    )(cols, vals, var, mean, source, *xs, *ys, after)


def split(x):
    hi = x.astype(jnp.bfloat16)
    return hi, (x - hi.astype(jnp.float32)).astype(jnp.bfloat16)


def mxu(a, b):
    return jnp.dot(a, b, preferred_element_type=jnp.float32)


def sweep_kernel(nb, cols_ref, vals_ref, var_ref, mean_ref, source_ref, u_ref, v_ref, vt_ref, g_ref, rs_ref, *refs):
    blocks, refs = refs[:nb], refs[nb:]
    out_ref, keep_ref, send_ref, full_ref, lap_ref, t_ref, hi_ref, lo_ref = refs
    n, X, Y, Z = u_ref.shape
    K = var_ref.shape[0]
    me = lax.axis_index("chaos")
    fill_slots(me, blocks, full_ref)
    mean = mean_ref[...]
    inv = 1.0 / (9.0 * mean)

    def row(i, carry):
        acc = mixed_row(i, n, cols_ref, vals_ref, full_ref, var_ref)
        first = source_ref[i] - (mean * blocks[0][i] + acc)
        keep = jnp.where(me * n + i < P_SIZE, 1.0, 0.0)
        out_ref[i] = keep * (u_ref[i] + first * inv)
        return carry

    lax.fori_loop(0, n, row, 0)

    sub = lax.broadcasted_iota(jnp.int32, (Y, Z), 0)
    lane = lax.broadcasted_iota(jnp.int32, (Y, Z), 1)
    R = X * Y
    for s in range(n):
        plane = [out_ref[s, x] for x in range(X)]
        for x in range(X):
            v = plane[x]
            near = jnp.where(sub == 0, 0.0, pltpu.roll(v, 1, 0)) + jnp.where(sub == Y - 1, 0.0, pltpu.roll(v, Y - 1, 0))
            near += jnp.where(lane == 0, 0.0, pltpu.roll(v, 1, 1)) + jnp.where(lane == Z - 1, 0.0, pltpu.roll(v, Z - 1, 1))
            if x:
                near += plane[x - 1]
            if x + 1 < X:
                near += plane[x + 1]
            lap_ref[s * R + x * Y:s * R + (x + 1) * Y, :] = 6.0 * v - near
    at = row_list(X, Y)
    J = whole_groups(n)
    flat = out_ref.reshape(n * R, Z)

    def beside(x, y):
        inside = min(max(x, 0), X - 1) * Y + min(max(y, 0), Y - 1)
        return (lap_ref if (0 <= x < X and 0 <= y < Y) else flat), inside

    for (x, y), e in at.items():
        ref, r = beside(x, y)
        t_ref[e] = ref[pl.ds(r, J, stride=R), :]

    B = Y // 2 + 2

    def put(sums, where):
        for (a, b), q in sums.items():
            hi, lo = split(jnp.zeros((16, Z), jnp.float32) if q is None else q)
            c = ((a + 1) * B + b + 1) * Z
            hi_ref[where, c:c + Z] = hi
            lo_ref[where, c:c + Z] = lo

    def variable(k, carry):
        for g in range(J // 16):
            sums = coarse_sums(X, Y, lambda x, y: v_ref[k, pl.ds(at[x, y], 1), :] * t_ref[at[x, y], 16 * g:16 * g + 16, :])
            put(sums, pl.ds(pl.multiple_of(k * J + 16 * g, 16), 16))
        return carry

    lax.fori_loop(0, K + 1, variable, 0)
    for j in range(J, n):
        def term(x, y):
            ref, r = beside(x, y)
            return vt_ref[at[x, y]] * ref[j * R + r:j * R + r + 1, :]
        start = (K + 1) * J + 16 * (j - J)
        put(coarse_sums(X, Y, term), slice(start, start + 16))

    step = rs_ref.shape[0]
    M = g_ref.shape[0] // 2
    c = lax.broadcasted_iota(jnp.int32, (2 * Z, Z), 1)
    z = lax.broadcasted_iota(jnp.int32, (2 * Z, Z), 0)
    half = Z // 2
    mid = jnp.where(c < half, 2 * c, Z + 2 * (c - half))
    same = (c < half) == (z < Z)
    weight = jnp.where(z == mid, 0.5, jnp.where(jnp.logical_and(same, jnp.abs(z - mid) == 1), 0.25, 0.0))
    weight = weight.astype(jnp.bfloat16)
    g_all, g_hi = g_ref[...], g_ref[0:M, :]
    pairs = B // 2
    for a in range(X // 2 + 2):
        for m in range(pairs):
            lanes = slice((a * B + 2 * m) * Z, (a * B + 2 * m + 2) * Z)
            both = mxu(g_all, hi_ref[:, lanes])
            mixed = both[:M] + both[M:] + mxu(g_hi, lo_ref[:, lanes])
            mixed = jnp.concatenate([mixed[:step] + rs_ref[:, lanes], mixed[step:]], 0)
            hi, lo = split(mixed)
            part = mxu(hi, weight) + mxu(lo, weight)
            for p in range(nb):
                ref = send_ref if p % 2 else keep_ref
                ref[p // 2, a, m * n:(m + 1) * n, :] = part[p * step:p * step + n]


def sweep(cols, vals, var, mean, source, u, tables, blocks):
    n, X, Y, Z = u.shape
    nb = len(blocks)
    v, vt, g, rs = tables
    rows = v.shape[1]
    part = jax.ShapeDtypeStruct((nb // 2, X // 2 + 2, (Y // 2 + 2) // 2 * n, Z), u.dtype)
    return pl.pallas_call(
        functools.partial(sweep_kernel, nb),
        out_shape=[jax.ShapeDtypeStruct(u.shape, u.dtype), part, part],
        in_specs=[SMEM, SMEM] + [VMEM] * (8 + nb),
        out_specs=[VMEM] * 3,
        scratch_shapes=[pltpu.VMEM((n * nb, X, Y, Z), jnp.float32),
                        pltpu.VMEM((n * X * Y, Z), jnp.float32),
                        pltpu.VMEM((rows, whole_groups(n), Z), jnp.float32),
                        pltpu.VMEM((g.shape[1], rs.shape[1]), jnp.bfloat16),
                        pltpu.VMEM((g.shape[1], rs.shape[1]), jnp.bfloat16)],
        compiler_params=PARAMS,
        name="sweep",
    )(cols, vals, var, mean, source, u, v, vt, g, rs, *blocks)


def final_kernel(ny, main_ref, *refs):
    ys, out_ref = refs[:ny], refs[ny]
    n, A, B, H = out_ref.shape
    fy = side_flags("gy")
    lane = lax.broadcasted_iota(jnp.int32, (n, 2 * H), 1)
    pairs = B // 2 + 1
    for a in range(A):
        low = sum(f[0] * r[a] for f, r in zip(fy, ys))
        high = sum(f[1] * r[a] for f, r in zip(fy, ys))
        part = [main_ref[a, m * n:(m + 1) * n, :] for m in range(pairs)]
        part[0] = part[0] + low
        part[-1] = part[-1] + high
        for b in range(B):
            v = part[(b + 1) // 2]
            if b % 2 == 0:
                v = pltpu.roll(v, H, 1)
            out_ref[:, a, b, :] = v[:, :H]


def final(main, ys, shape):
    return pl.pallas_call(
        functools.partial(final_kernel, len(ys)),
        out_shape=jax.ShapeDtypeStruct(shape, main.dtype),
        in_specs=[VMEM] * (1 + len(ys)),
        out_specs=VMEM,
        compiler_params=PARAMS,
        name="final",
    )(main, *ys)


def body(field, source, mean_coef, var_coefs, galerkin_cols, galerkin_vals):
    n, X, Y, Z = field.shape
    P = lax.axis_size("chaos")
    gx = lax.axis_size("gx")

    xs = swap_sides(field[:, 0], field[:, X - 1], "gx")
    ys = swap_sides(field[:, :, 0], field[:, :, Y - 1], "gy")
    lap = laplace(field, xs, ys)
    blocks = gather_blocks(lap)

    cols_all, vals_all, var_now, mean_now, lap_now = lax.optimization_barrier(
        (galerkin_cols, galerkin_vals, var_coefs, mean_coef, lap))
    first_row = lax.axis_index("chaos") * n
    cols = lax.dynamic_slice_in_dim(cols_all, first_row, n, 1).reshape(-1)
    vals = lax.dynamic_slice_in_dim(vals_all, first_row, n, 1).reshape(-1)
    both = jnp.concatenate([var_now, mean_now[None]], 0)
    vx = swap_sides(both[:, 0], both[:, X - 1], "gx")
    vy = swap_sides(both[:, :, 0], both[:, :, Y - 1], "gy")
    tables = prep(P, jnp.transpose(cols_all, (0, 2, 1)), jnp.transpose(vals_all, (0, 2, 1)), var_coefs, mean_coef,
                  source, vx, vy, lap_now[:1, 0])
    smoothed, keep, send = sweep(cols, vals, var_coefs, mean_coef, source, field, tables, blocks)

    d = 1
    parts = keep + lax.ppermute(send, "chaos", [(i, i ^ 1) for i in range(P)])
    main, edge_lo, edge_hi = parts[:, 1:-1], parts[:, 0], parts[:, -1]
    even = lax.axis_index("gx") % 2 == 0
    total = main[0]
    far = [(q, lax.ppermute(main[q], "chaos", [(i, i ^ (2 * q)) for i in range(P)])) for q in range(1, P // 2)]
    sides = []
    for p in range(phases(gx)):
        up = even if p == 0 else jnp.logical_not(even)
        edge = jnp.where(up, edge_hi, edge_lo)
        got = None
        for q in range(P // 2):
            pairs = [(i * P + j, partner(i, p, gx) * P + (j ^ (2 * q))) for i in range(gx) for j in range(P)]
            r = lax.ppermute(edge[q], ("gx", "chaos"), pairs)
            got = r if got is None else got + r
        sides.append(got)
    for q, r in far:
        total = total + r
    flags = side_flags("gx")
    low = sum(f[0] * r for f, r in zip(flags, sides))
    high = sum(f[1] * r for f, r in zip(flags, sides))
    A = total.shape[0]
    total = jnp.concatenate([total[:1] + low[None], total[1:]], 0)
    total = jnp.concatenate([total[:-1], total[-1:] + high[None]], 0)

    half = Z // 2
    lane = lax.broadcasted_iota(jnp.int32, (1, 1, Z), 2)
    low_rows = jnp.where(lane < half, total[:, :n], 0.0)
    high_rows = jnp.where(lane < half, 0.0, total[:, -n:])
    ys = swap_sides(low_rows, high_rows, "gy")
    coarse = final(total, ys, (n, A, Y // 2, half))
    return smoothed, coarse


def solution(mesh):
    return jax.shard_map(
        body,
        mesh=mesh,
        in_specs=(
            P("chaos", "gx", "gy", None),
            P("chaos", "gx", "gy", None),
            P("gx", "gy", None),
            P(None, "gx", "gy", None),
            P(),
            P(),
        ),
        out_specs=(P("chaos", "gx", "gy", None), P("chaos", "gx", "gy", None)),
        check_vma=False,
    )
```

```python
import functools

import jax
import jax.numpy as jnp
from jax import lax
from jax.experimental import pallas as pl
from jax.experimental.pallas import tpu as pltpu
from jax.sharding import PartitionSpec as P

P_SIZE = 66
PARAMS = pltpu.CompilerParams(vmem_limit_bytes=12 << 20)
VMEM = pl.BlockSpec(memory_space=pltpu.VMEM)
SMEM = pl.BlockSpec(memory_space=pltpu.SMEM)


def partner(i, phase, n):
    j = i + 1 if i % 2 == phase else i - 1
    return j if 0 <= j < n else i


def pair_pairs(phase, n):
    return [(i, partner(i, phase, n)) for i in range(n)]


def phases(n):
    return 1 if n == 2 else 2


def swap_sides(low, high, axis):
    n = lax.axis_size(axis)
    even = lax.axis_index(axis) % 2 == 0
    picks = [jnp.where(even, high, low), jnp.where(even, low, high)]
    return [lax.ppermute(picks[p], axis, pair_pairs(p, n)) for p in range(phases(n))]


def side_flags(axis):
    n = lax.axis_size(axis)
    i = lax.axis_index(axis)
    odd = lax.rem(i, 2)
    flags = []
    for p in range(phases(n)):
        up = jnp.logical_and(odd == p, i + 1 < n)
        down = jnp.logical_and(odd != p, i > 0)
        flags.append((jnp.where(down, 1.0, 0.0), jnp.where(up, 1.0, 0.0)))
    return flags


def edges_kernel(nx, ny, u_ref, var_ref, mean_ref, *refs):
    xs, ys = refs[:nx], refs[nx:]
    n, X, Y, Z = u_ref.shape
    K = var_ref.shape[0]
    even = [lax.rem(lax.axis_index(axis), 2) == 0 for axis in ("gx", "gy")]
    for p, ref in enumerate(xs):
        at = jnp.where(even[0] if p == 0 else jnp.logical_not(even[0]), X - 1, 0)
        for s in range(n):
            ref[s] = u_ref[s, at]
        for k in range(K):
            ref[n + k] = var_ref[k, at]
        ref[n + K] = mean_ref[at]
    flag = jnp.where(even[1], 1.0, 0.0)
    for src, where in ((u_ref, slice(0, n)), (var_ref, slice(n, n + K))):
        low, high = src[:, :, 0, :], src[:, :, Y - 1, :]
        for p, ref in enumerate(ys):
            f = flag if p == 0 else 1.0 - flag
            ref[where] = f * high + (1.0 - f) * low
    low, high = mean_ref[:, 0, :], mean_ref[:, Y - 1, :]
    for p, ref in enumerate(ys):
        f = flag if p == 0 else 1.0 - flag
        ref[n + K] = f * high + (1.0 - f) * low


def edges(u, var, mean, nx, ny):
    n, X, Y, Z = u.shape
    planes = n + var.shape[0] + 1
    out = [jax.ShapeDtypeStruct((planes, Y, Z), u.dtype)] * nx + [jax.ShapeDtypeStruct((planes, X, Z), u.dtype)] * ny
    res = pl.pallas_call(
        functools.partial(edges_kernel, nx, ny),
        out_shape=out,
        in_specs=[VMEM] * 3,
        out_specs=[VMEM] * len(out),
        compiler_params=PARAMS,
        name="edges",
    )(u, var, mean)
    return res[:nx], res[nx:]


def lap_kernel(nx, ny, u_ref, *refs):
    xs, ys, out_ref = refs[:nx], refs[nx:nx + ny], refs[nx + ny]
    n, X, Y, Z = u_ref.shape
    fx, fy = side_flags("gx"), side_flags("gy")
    sub = lax.broadcasted_iota(jnp.int32, (Y, Z), 0)
    lane = lax.broadcasted_iota(jnp.int32, (Y, Z), 1)
    for s in range(n):
        plane = [u_ref[s, x] for x in range(X)]
        below = sum(f[0] * r[s] for f, r in zip(fx, xs))
        above = sum(f[1] * r[s] for f, r in zip(fx, xs))
        row_lo = sum(f[0] * r[s] for f, r in zip(fy, ys))
        row_hi = sum(f[1] * r[s] for f, r in zip(fy, ys))
        for x in range(X):
            v = plane[x]
            near = (plane[x - 1] if x else below) + (plane[x + 1] if x + 1 < X else above)
            near += jnp.where(sub == 0, row_lo[x:x + 1], pltpu.roll(v, 1, 0))
            near += jnp.where(sub == Y - 1, row_hi[x:x + 1], pltpu.roll(v, Y - 1, 0))
            near += jnp.where(lane == 0, 0.0, pltpu.roll(v, 1, 1))
            near += jnp.where(lane == Z - 1, 0.0, pltpu.roll(v, Z - 1, 1))
            out_ref[s, x] = 6.0 * v - near


def laplace(u, xs, ys):
    return pl.pallas_call(
        functools.partial(lap_kernel, len(xs), len(ys)),
        out_shape=jax.ShapeDtypeStruct(u.shape, u.dtype),
        in_specs=[VMEM] * (1 + len(xs) + len(ys)),
        out_specs=VMEM,
        compiler_params=PARAMS,
        name="laplace",
    )(u, *xs, *ys)


def gather_blocks(own, beside):
    n = lax.axis_size("chaos")
    blocks = {0: own}
    d = n // 2
    extra = None
    while d:
        for p in list(blocks):
            block = blocks[p]
            if p and extra is None:
                extra = beside()
                block, extra = lax.optimization_barrier((block, extra))
            blocks[p ^ d] = lax.ppermute(block, "chaos", [(i, i ^ d) for i in range(n)])
        d //= 2
    return [blocks[p] for p in range(n)], extra


def fill_slots(me, blocks, full_ref):
    n = blocks[0].shape[0]
    for p, ref in enumerate(blocks):
        base = (me ^ p) * n
        for s in range(n):
            full_ref[base + s] = ref[s]


def mixed_row(i, n, cols_ref, vals_ref, full_ref, var_ref):
    K = var_ref.shape[0]
    nb = cols_ref.shape[0] // (K * n)
    acc = None
    for k in range(K):
        m = None
        for b in range(nb):
            at = (k * n + i) * nb + b
            t = vals_ref[at] * full_ref[cols_ref[at]]
            m = t if m is None else m + t
        m = var_ref[k] * m
        acc = m if acc is None else acc + m
    return acc


def row_list(X, Y):
    at = {(x, y): x * Y + y for x in range(X) for y in range(Y)}
    base = X * Y
    at.update({(-1, y): base + y for y in range(Y)})
    at.update({(X, y): base + Y + y for y in range(Y)})
    at.update({(x, -1): base + 2 * Y + x for x in range(X)})
    at.update({(x, Y): base + 2 * Y + X + x for x in range(X)})
    return at


def coarse_sums(X, Y, term):
    cols = {}
    for x in range(-1, X + 1):
        ys = [y for y in range(-1, Y + 1) if 0 <= x < X or 0 <= y < Y]
        got = {y: term(x, y) for y in ys}
        for b in range(-1, Y // 2 + 1):
            taps = [got[y] for y in (2 * b - 1, 2 * b, 2 * b + 1) if got.get(y) is not None]
            if taps:
                cols[x, b] = functools.reduce(jnp.add, taps)
    out = {}
    for a in range(-1, X // 2 + 1):
        for b in range(-1, Y // 2 + 1):
            taps = [cols[x, b] for x in (2 * a - 1, 2 * a, 2 * a + 1) if (x, b) in cols]
            out[a, b] = functools.reduce(jnp.add, taps) if taps else None
    return out


def whole_groups(n):
    return n // 16 * 16


def prep_kernel(P, nx, ny, cols_ref, vals_ref, var_ref, mean_ref, source_ref, *refs):
    xs, ys = refs[:nx], refs[nx:nx + ny]
    v_ref, vt_ref, g_ref, rs_ref, gt_ref = refs[nx + ny + 1:]
    n, X, Y, Z = source_ref.shape
    K = var_ref.shape[0]
    J = whole_groups(n)
    me = lax.axis_index("chaos")
    wide = cols_ref.shape[2]

    fx, fy = side_flags("gx"), side_flags("gy")
    sub = lax.broadcasted_iota(jnp.int32, (Y, Z), 0)
    wy = jnp.where(lax.rem(sub, 2) == 0, 0.5, 0.25)
    base = X * Y
    for k in range(K + 1):
        for x in range(X):
            plane = var_ref[k, x] if k < K else mean_ref[x]
            v_ref[k, x * Y:(x + 1) * Y, :] = plane * (-(0.5 if x % 2 == 0 else 0.25) * wy)
        low = sum(f[0] * r[n + k] for f, r in zip(fx, xs))
        high = sum(f[1] * r[n + k] for f, r in zip(fx, xs))
        v_ref[k, base:base + Y, :] = low * (0.25 * wy)
        v_ref[k, base + Y:base + 2 * Y, :] = high * (0.5 * wy)
        low = sum(f[0] * r[n + k] for f, r in zip(fy, ys))
        high = sum(f[1] * r[n + k] for f, r in zip(fy, ys))
        wx = jnp.where(lax.rem(lax.broadcasted_iota(jnp.int32, (X, Z), 0), 2) == 0, 0.5, 0.25)
        v_ref[k, base + 2 * Y:base + 2 * Y + X, :] = low * (0.25 * wx)
        v_ref[k, base + 2 * Y + X:base + 2 * Y + 2 * X, :] = high * (0.5 * wx)
    rows = base + 2 * Y + 2 * X
    vt_ref[...] = jnp.zeros_like(vt_ref)
    for k in range(K + 1):
        for e in range(rows // 8):
            vt_ref[8 * e:8 * e + 8, k, :] = v_ref[k, 8 * e:8 * e + 8, :]

    gt_ref[...] = jnp.zeros_like(gt_ref)
    first = me * n
    slot = lax.broadcasted_iota(jnp.int32, (J, wide), 0) + first
    lane = lax.broadcasted_iota(jnp.int32, (J, wide), 1)
    for k in range(K + 1):
        if k < K:
            c, v = cols_ref[k], vals_ref[k]
            v = jnp.where(lax.broadcasted_iota(jnp.int32, v.shape, 1) < P_SIZE, v, 0.0)
            hits = sum(jnp.where(c[b:b + 1] == slot, v[b:b + 1], 0.0) for b in range(c.shape[0]))
            rest = [sum(jnp.where(c[b:b + 1] == first + j, v[b:b + 1], 0.0) for b in range(c.shape[0]))
                    for j in range(J, n)]
        else:
            hits = jnp.where(lane == slot, 1.0, 0.0)
            rest = [jnp.where(lane[:1] == first + j, 1.0, 0.0) for j in range(J, n)]
        gt_ref[k * J:(k + 1) * J, 0:wide] = hits
        for j, r in enumerate(rest):
            at = (K + 1) * J + 16 * j + k
            gt_ref[at:at + 1, 0:wide] = r
    gt = gt_ref[...]
    lanes = lax.broadcasted_iota(jnp.int32, gt.shape, 1)
    total = gt.shape[1]
    step = (n + 7) // 8 * 8
    picked = jnp.zeros_like(gt)
    for p in range(P):
        shift = lax.rem(p * step - (me ^ p) * n + 8 * total, total)
        moved = pltpu.roll(gt, shift, 1)
        picked = jnp.where(jnp.logical_and(lanes >= p * step, lanes < p * step + n), moved, picked)
    g = jnp.transpose(picked)[:P * step]
    depth = g_ref.shape[1]
    hi = g.astype(jnp.bfloat16)
    lo = (g - hi.astype(jnp.float32)).astype(jnp.bfloat16)
    g_ref[0:P * step, :] = hi[:, :depth]
    g_ref[P * step:2 * P * step, :] = lo[:, :depth]

    flat = source_ref.reshape(n * X * Y, Z)
    keep = jnp.where(lax.broadcasted_iota(jnp.int32, (n, Z), 0) + first < P_SIZE, 1.0, 0.0)

    def term(x, y):
        if not (0 <= x < X and 0 <= y < Y):
            return None
        w = (0.5 if x % 2 == 0 else 0.25) * (0.5 if y % 2 == 0 else 0.25)
        return flat[pl.ds(x * Y + y, n, stride=X * Y), :] * (w * keep)

    rs_ref[...] = jnp.zeros_like(rs_ref)
    B = Y // 2 + 2
    for (a, b), t in coarse_sums(X, Y, term).items():
        if t is not None:
            at = ((a + 1) * B + b + 1) * Z
            rs_ref[0:n, at:at + Z] = t


def prep(P, cols, vals, var, mean, source, xs, ys, after):
    n, X, Y, Z = source.shape
    K = var.shape[0]
    rows = X * Y + 2 * Y + 2 * X
    depth = (K + 1) * whole_groups(n) + 16 * (n - whole_groups(n))
    step = (n + 7) // 8 * 8
    wide = (X // 2 + 2) * (Y // 2 + 2) * Z
    return pl.pallas_call(
        functools.partial(prep_kernel, P, len(xs), len(ys)),
        out_shape=[jax.ShapeDtypeStruct((K + 1, rows, Z), jnp.float32),
                   jax.ShapeDtypeStruct((rows, 16, Z), jnp.float32),
                   jax.ShapeDtypeStruct((2 * P * step, depth), jnp.bfloat16),
                   jax.ShapeDtypeStruct((step, wide), jnp.float32)],
        in_specs=[VMEM] * (6 + len(xs) + len(ys)),
        out_specs=[VMEM] * 4,
        scratch_shapes=[pltpu.VMEM(((depth + 127) // 128 * 128, (P * step + 127) // 128 * 128), jnp.float32)],
        compiler_params=PARAMS,
        name="prep",
    )(cols, vals, var, mean, source, *xs, *ys, after)


def split(x):
    hi = x.astype(jnp.bfloat16)
    return hi, (x - hi.astype(jnp.float32)).astype(jnp.bfloat16)


def mxu(a, b):
    return jnp.dot(a, b, preferred_element_type=jnp.float32)


def sweep_kernel(nb, cols_ref, vals_ref, var_ref, mean_ref, source_ref, u_ref, v_ref, vt_ref, g_ref, rs_ref, *refs):
    blocks, refs = refs[:nb], refs[nb:]
    out_ref, keep_ref, send_ref, full_ref, lap_ref, t_ref, hi_ref, lo_ref = refs
    n, X, Y, Z = u_ref.shape
    K = var_ref.shape[0]
    me = lax.axis_index("chaos")
    fill_slots(me, blocks, full_ref)
    mean = mean_ref[...]
    inv = 1.0 / (9.0 * mean)

    def row(i, carry):
        acc = mixed_row(i, n, cols_ref, vals_ref, full_ref, var_ref)
        first = source_ref[i] - (mean * blocks[0][i] + acc)
        keep = jnp.where(me * n + i < P_SIZE, 1.0, 0.0)
        out_ref[i] = keep * (u_ref[i] + first * inv)
        return carry

    lax.fori_loop(0, n, row, 0)

    sub = lax.broadcasted_iota(jnp.int32, (Y, Z), 0)
    lane = lax.broadcasted_iota(jnp.int32, (Y, Z), 1)
    R = X * Y
    for s in range(n):
        plane = [out_ref[s, x] for x in range(X)]
        for x in range(X):
            v = plane[x]
            near = jnp.where(sub == 0, 0.0, pltpu.roll(v, 1, 0)) + jnp.where(sub == Y - 1, 0.0, pltpu.roll(v, Y - 1, 0))
            near += jnp.where(lane == 0, 0.0, pltpu.roll(v, 1, 1)) + jnp.where(lane == Z - 1, 0.0, pltpu.roll(v, Z - 1, 1))
            if x:
                near += plane[x - 1]
            if x + 1 < X:
                near += plane[x + 1]
            lap_ref[s * R + x * Y:s * R + (x + 1) * Y, :] = 6.0 * v - near
    at = row_list(X, Y)
    J = whole_groups(n)
    flat = out_ref.reshape(n * R, Z)

    def beside(x, y):
        inside = min(max(x, 0), X - 1) * Y + min(max(y, 0), Y - 1)
        return (lap_ref if (0 <= x < X and 0 <= y < Y) else flat), inside

    for (x, y), e in at.items():
        ref, r = beside(x, y)
        t_ref[e] = ref[pl.ds(r, J, stride=R), :]

    B = Y // 2 + 2

    def put(sums, where):
        for (a, b), q in sums.items():
            hi, lo = split(jnp.zeros((16, Z), jnp.float32) if q is None else q)
            c = ((a + 1) * B + b + 1) * Z
            hi_ref[where, c:c + Z] = hi
            lo_ref[where, c:c + Z] = lo

    def variable(k, carry):
        for g in range(J // 16):
            sums = coarse_sums(X, Y, lambda x, y: v_ref[k, pl.ds(at[x, y], 1), :] * t_ref[at[x, y], 16 * g:16 * g + 16, :])
            put(sums, pl.ds(pl.multiple_of(k * J + 16 * g, 16), 16))
        return carry

    lax.fori_loop(0, K + 1, variable, 0)
    for j in range(J, n):
        def term(x, y):
            ref, r = beside(x, y)
            return vt_ref[at[x, y]] * ref[j * R + r:j * R + r + 1, :]
        start = (K + 1) * J + 16 * (j - J)
        put(coarse_sums(X, Y, term), slice(start, start + 16))

    step = rs_ref.shape[0]
    M = g_ref.shape[0] // 2
    c = lax.broadcasted_iota(jnp.int32, (2 * Z, Z), 1)
    z = lax.broadcasted_iota(jnp.int32, (2 * Z, Z), 0)
    half = Z // 2
    mid = jnp.where(c < half, 2 * c, Z + 2 * (c - half))
    same = (c < half) == (z < Z)
    weight = jnp.where(z == mid, 0.5, jnp.where(jnp.logical_and(same, jnp.abs(z - mid) == 1), 0.25, 0.0))
    weight = weight.astype(jnp.bfloat16)
    g_all, g_hi = g_ref[...], g_ref[0:M, :]
    pairs = B // 2
    for a in range(X // 2 + 2):
        for m in range(pairs):
            lanes = slice((a * B + 2 * m) * Z, (a * B + 2 * m + 2) * Z)
            both = mxu(g_all, hi_ref[:, lanes])
            mixed = both[:M] + both[M:] + mxu(g_hi, lo_ref[:, lanes])
            mixed = jnp.concatenate([mixed[:step] + rs_ref[:, lanes], mixed[step:]], 0)
            hi, lo = split(mixed)
            part = mxu(hi, weight) + mxu(lo, weight)
            for p in range(nb):
                ref = send_ref if p % 2 else keep_ref
                ref[p // 2, a, m * n:(m + 1) * n, :] = part[p * step:p * step + n]


def sweep(cols, vals, var, mean, source, u, tables, blocks):
    n, X, Y, Z = u.shape
    nb = len(blocks)
    v, vt, g, rs = tables
    rows = v.shape[1]
    part = jax.ShapeDtypeStruct((nb // 2, X // 2 + 2, (Y // 2 + 2) // 2 * n, Z), u.dtype)
    return pl.pallas_call(
        functools.partial(sweep_kernel, nb),
        out_shape=[jax.ShapeDtypeStruct(u.shape, u.dtype), part, part],
        in_specs=[SMEM, SMEM] + [VMEM] * (8 + nb),
        out_specs=[VMEM] * 3,
        scratch_shapes=[pltpu.VMEM((n * nb, X, Y, Z), jnp.float32),
                        pltpu.VMEM((n * X * Y, Z), jnp.float32),
                        pltpu.VMEM((rows, whole_groups(n), Z), jnp.float32),
                        pltpu.VMEM((g.shape[1], rs.shape[1]), jnp.bfloat16),
                        pltpu.VMEM((g.shape[1], rs.shape[1]), jnp.bfloat16)],
        compiler_params=PARAMS,
        name="sweep",
    )(cols, vals, var, mean, source, u, v, vt, g, rs, *blocks)


def final_kernel(ny, main_ref, *refs):
    ys, out_ref = refs[:ny], refs[ny]
    n, A, B, H = out_ref.shape
    fy = side_flags("gy")
    lane = lax.broadcasted_iota(jnp.int32, (n, 2 * H), 1)
    pairs = B // 2 + 1
    for a in range(A):
        low = sum(f[0] * r[a] for f, r in zip(fy, ys))
        high = sum(f[1] * r[a] for f, r in zip(fy, ys))
        part = [main_ref[a, m * n:(m + 1) * n, :] for m in range(pairs)]
        part[0] = part[0] + low
        part[-1] = part[-1] + high
        for b in range(B):
            v = part[(b + 1) // 2]
            if b % 2 == 0:
                v = pltpu.roll(v, H, 1)
            out_ref[:, a, b, :] = v[:, :H]


def final(main, ys, shape):
    return pl.pallas_call(
        functools.partial(final_kernel, len(ys)),
        out_shape=jax.ShapeDtypeStruct(shape, main.dtype),
        in_specs=[VMEM] * (1 + len(ys)),
        out_specs=VMEM,
        compiler_params=PARAMS,
        name="final",
    )(main, *ys)


def body(field, source, mean_coef, var_coefs, galerkin_cols, galerkin_vals):
    n, X, Y, Z = field.shape
    P = lax.axis_size("chaos")
    gx = lax.axis_size("gx")

    gy = lax.axis_size("gy")
    xs, ys = edges(field, var_coefs, mean_coef, phases(gx), phases(gy))
    xs = [lax.ppermute(v, "gx", pair_pairs(p, gx)) for p, v in enumerate(xs)]
    ys = [lax.ppermute(v, "gy", pair_pairs(p, gy)) for p, v in enumerate(ys)]
    lap = laplace(field, xs, ys)

    def beside():
        cols_all, vals_all, lap_now = lax.optimization_barrier((galerkin_cols, galerkin_vals, lap))
        first_row = lax.axis_index("chaos") * n
        cols = lax.dynamic_slice_in_dim(cols_all, first_row, n, 1).reshape(-1)
        vals = lax.dynamic_slice_in_dim(vals_all, first_row, n, 1).reshape(-1)
        tables = prep(P, jnp.transpose(cols_all, (0, 2, 1)), jnp.transpose(vals_all, (0, 2, 1)), var_coefs, mean_coef,
                      source, xs, ys, lap_now[:1, 0])
        return cols, vals, tables

    blocks, (cols, vals, tables) = gather_blocks(lap, beside)
    smoothed, keep, send = sweep(cols, vals, var_coefs, mean_coef, source, field, tables, blocks)

    parts = keep + lax.ppermute(send, "chaos", [(i, i ^ 1) for i in range(P)])
    main, edge_lo, edge_hi = parts[:, 1:-1], parts[:, 0], parts[:, -1]
    even = lax.axis_index("gx") % 2 == 0
    total = main[0]
    far = [(q, lax.ppermute(main[q], "chaos", [(i, i ^ (2 * q)) for i in range(P)])) for q in range(1, P // 2)]
    sides = []
    for p in range(phases(gx)):
        up = even if p == 0 else jnp.logical_not(even)
        edge = jnp.where(up, edge_hi, edge_lo)
        got = None
        for q in range(P // 2):
            pairs = [(i * P + j, partner(i, p, gx) * P + (j ^ (2 * q))) for i in range(gx) for j in range(P)]
            r = lax.ppermute(edge[q], ("gx", "chaos"), pairs)
            got = r if got is None else got + r
        sides.append(got)
    for q, r in far:
        total = total + r
    flags = side_flags("gx")
    low = sum(f[0] * r for f, r in zip(flags, sides))
    high = sum(f[1] * r for f, r in zip(flags, sides))
    A = total.shape[0]
    total = jnp.concatenate([total[:1] + low[None], total[1:]], 0)
    total = jnp.concatenate([total[:-1], total[-1:] + high[None]], 0)

    half = Z // 2
    lane = lax.broadcasted_iota(jnp.int32, (1, 1, Z), 2)
    low_rows = jnp.where(lane < half, total[:, :n], 0.0)
    high_rows = jnp.where(lane < half, 0.0, total[:, -n:])
    ys = swap_sides(low_rows, high_rows, "gy")
    coarse = final(total, ys, (n, A, Y // 2, half))
    return smoothed, coarse


def solution(mesh):
    return jax.shard_map(
        body,
        mesh=mesh,
        in_specs=(
            P("chaos", "gx", "gy", None),
            P("chaos", "gx", "gy", None),
            P("gx", "gy", None),
            P(None, "gx", "gy", None),
            P(),
            P(),
        ),
        out_specs=(P("chaos", "gx", "gy", None), P("chaos", "gx", "gy", None)),
        check_vma=False,
    )
```

```python
import functools

import jax
import jax.numpy as jnp
from jax import lax
from jax.experimental import pallas as pl
from jax.experimental.pallas import tpu as pltpu
from jax.sharding import PartitionSpec as P

P_SIZE = 66
PARAMS = pltpu.CompilerParams(vmem_limit_bytes=12 << 20)
VMEM = pl.BlockSpec(memory_space=pltpu.VMEM)
SMEM = pl.BlockSpec(memory_space=pltpu.SMEM)


def partner(i, phase, n):
    j = i + 1 if i % 2 == phase else i - 1
    return j if 0 <= j < n else i


def pair_pairs(phase, n):
    return [(i, partner(i, phase, n)) for i in range(n)]


def phases(n):
    return 1 if n == 2 else 2


def swap_sides(low, high, axis):
    n = lax.axis_size(axis)
    even = lax.axis_index(axis) % 2 == 0
    picks = [jnp.where(even, high, low), jnp.where(even, low, high)]
    return [lax.ppermute(picks[p], axis, pair_pairs(p, n)) for p in range(phases(n))]


def side_flags(axis):
    n = lax.axis_size(axis)
    i = lax.axis_index(axis)
    odd = lax.rem(i, 2)
    flags = []
    for p in range(phases(n)):
        up = jnp.logical_and(odd == p, i + 1 < n)
        down = jnp.logical_and(odd != p, i > 0)
        flags.append((jnp.where(down, 1.0, 0.0), jnp.where(up, 1.0, 0.0)))
    return flags


def edges_kernel(nx, ny, u_ref, var_ref, mean_ref, *refs):
    xs, ys = refs[:nx], refs[nx:]
    n, X, Y, Z = u_ref.shape
    K = var_ref.shape[0]
    even = [lax.rem(lax.axis_index(axis), 2) == 0 for axis in ("gx", "gy")]
    for p, ref in enumerate(xs):
        at = jnp.where(even[0] if p == 0 else jnp.logical_not(even[0]), X - 1, 0)
        for s in range(n):
            ref[s] = u_ref[s, at]
        for k in range(K):
            ref[n + k] = var_ref[k, at]
        ref[n + K] = mean_ref[at]
    flag = jnp.where(even[1], 1.0, 0.0)
    for src, where in ((u_ref, slice(0, n)), (var_ref, slice(n, n + K))):
        low, high = src[:, :, 0, :], src[:, :, Y - 1, :]
        for p, ref in enumerate(ys):
            f = flag if p == 0 else 1.0 - flag
            ref[where] = f * high + (1.0 - f) * low
    low, high = mean_ref[:, 0, :], mean_ref[:, Y - 1, :]
    for p, ref in enumerate(ys):
        f = flag if p == 0 else 1.0 - flag
        ref[n + K] = f * high + (1.0 - f) * low


def edges(u, var, mean, nx, ny):
    n, X, Y, Z = u.shape
    planes = n + var.shape[0] + 1
    out = [jax.ShapeDtypeStruct((planes, Y, Z), u.dtype)] * nx + [jax.ShapeDtypeStruct((planes, X, Z), u.dtype)] * ny
    res = pl.pallas_call(
        functools.partial(edges_kernel, nx, ny),
        out_shape=out,
        in_specs=[VMEM] * 3,
        out_specs=[VMEM] * len(out),
        compiler_params=PARAMS,
        name="edges",
    )(u, var, mean)
    return res[:nx], res[nx:]


def lap_kernel(nx, ny, u_ref, *refs):
    xs, ys, out_ref = refs[:nx], refs[nx:nx + ny], refs[nx + ny]
    n, X, Y, Z = u_ref.shape
    fx, fy = side_flags("gx"), side_flags("gy")
    sub = lax.broadcasted_iota(jnp.int32, (Y, Z), 0)
    lane = lax.broadcasted_iota(jnp.int32, (Y, Z), 1)
    for s in range(n):
        plane = [u_ref[s, x] for x in range(X)]
        below = sum(f[0] * r[s] for f, r in zip(fx, xs))
        above = sum(f[1] * r[s] for f, r in zip(fx, xs))
        row_lo = sum(f[0] * r[s] for f, r in zip(fy, ys))
        row_hi = sum(f[1] * r[s] for f, r in zip(fy, ys))
        for x in range(X):
            v = plane[x]
            near = (plane[x - 1] if x else below) + (plane[x + 1] if x + 1 < X else above)
            near += jnp.where(sub == 0, row_lo[x:x + 1], pltpu.roll(v, 1, 0))
            near += jnp.where(sub == Y - 1, row_hi[x:x + 1], pltpu.roll(v, Y - 1, 0))
            near += jnp.where(lane == 0, 0.0, pltpu.roll(v, 1, 1))
            near += jnp.where(lane == Z - 1, 0.0, pltpu.roll(v, Z - 1, 1))
            out_ref[s, x] = 6.0 * v - near


def laplace(u, xs, ys):
    return pl.pallas_call(
        functools.partial(lap_kernel, len(xs), len(ys)),
        out_shape=jax.ShapeDtypeStruct(u.shape, u.dtype),
        in_specs=[VMEM] * (1 + len(xs) + len(ys)),
        out_specs=VMEM,
        compiler_params=PARAMS,
        name="laplace",
    )(u, *xs, *ys)


def gather_blocks(own, beside):
    n = lax.axis_size("chaos")
    blocks = {0: own}
    d = n // 2
    extra = None
    while d:
        for p in list(blocks):
            block = blocks[p]
            if p and extra is None:
                extra = beside()
                block, extra = lax.optimization_barrier((block, extra))
            blocks[p ^ d] = lax.ppermute(block, "chaos", [(i, i ^ d) for i in range(n)])
        d //= 2
    return [blocks[p] for p in range(n)], extra


def fill_slots(me, blocks, full_ref):
    n = blocks[0].shape[0]
    for p, ref in enumerate(blocks):
        base = (me ^ p) * n
        for s in range(n):
            full_ref[base + s] = ref[s]


def mixed_row(i, n, cols_ref, vals_ref, full_ref, var_ref):
    K = var_ref.shape[0]
    nb = cols_ref.shape[0] // (K * n)
    acc = None
    for k in range(K):
        m = None
        for b in range(nb):
            at = (k * n + i) * nb + b
            t = vals_ref[at] * full_ref[cols_ref[at]]
            m = t if m is None else m + t
        m = var_ref[k] * m
        acc = m if acc is None else acc + m
    return acc


def row_list(X, Y):
    at = {(x, y): x * Y + y for x in range(X) for y in range(Y)}
    base = X * Y
    at.update({(-1, y): base + y for y in range(Y)})
    at.update({(X, y): base + Y + y for y in range(Y)})
    at.update({(x, -1): base + 2 * Y + x for x in range(X)})
    at.update({(x, Y): base + 2 * Y + X + x for x in range(X)})
    return at


def coarse_sums(X, Y, term):
    cols = {}
    for x in range(-1, X + 1):
        ys = [y for y in range(-1, Y + 1) if 0 <= x < X or 0 <= y < Y]
        got = {y: term(x, y) for y in ys}
        for b in range(-1, Y // 2 + 1):
            taps = [got[y] for y in (2 * b - 1, 2 * b, 2 * b + 1) if got.get(y) is not None]
            if taps:
                cols[x, b] = functools.reduce(jnp.add, taps)
    out = {}
    for a in range(-1, X // 2 + 1):
        for b in range(-1, Y // 2 + 1):
            taps = [cols[x, b] for x in (2 * a - 1, 2 * a, 2 * a + 1) if (x, b) in cols]
            out[a, b] = functools.reduce(jnp.add, taps) if taps else None
    return out


def whole_groups(n):
    return n // 16 * 16


def prep_kernel(P, nx, ny, cols_ref, vals_ref, var_ref, mean_ref, source_ref, *refs):
    xs, ys = refs[:nx], refs[nx:nx + ny]
    v_ref, vt_ref, g_ref, rs_ref, gt_ref = refs[nx + ny + 1:]
    n, X, Y, Z = source_ref.shape
    K = var_ref.shape[0]
    J = whole_groups(n)
    me = lax.axis_index("chaos")
    wide = cols_ref.shape[2]

    fx, fy = side_flags("gx"), side_flags("gy")
    sub = lax.broadcasted_iota(jnp.int32, (Y, Z), 0)
    wy = jnp.where(lax.rem(sub, 2) == 0, 0.5, 0.25)
    base = X * Y
    for k in range(K + 1):
        for x in range(X):
            plane = var_ref[k, x] if k < K else mean_ref[x]
            v_ref[k, x * Y:(x + 1) * Y, :] = plane * (-(0.5 if x % 2 == 0 else 0.25) * wy)
        low = sum(f[0] * r[n + k] for f, r in zip(fx, xs))
        high = sum(f[1] * r[n + k] for f, r in zip(fx, xs))
        v_ref[k, base:base + Y, :] = low * (0.25 * wy)
        v_ref[k, base + Y:base + 2 * Y, :] = high * (0.5 * wy)
        low = sum(f[0] * r[n + k] for f, r in zip(fy, ys))
        high = sum(f[1] * r[n + k] for f, r in zip(fy, ys))
        wx = jnp.where(lax.rem(lax.broadcasted_iota(jnp.int32, (X, Z), 0), 2) == 0, 0.5, 0.25)
        v_ref[k, base + 2 * Y:base + 2 * Y + X, :] = low * (0.25 * wx)
        v_ref[k, base + 2 * Y + X:base + 2 * Y + 2 * X, :] = high * (0.5 * wx)
    rows = base + 2 * Y + 2 * X
    vt_ref[...] = jnp.zeros_like(vt_ref)
    for k in range(K + 1):
        for e in range(rows // 8):
            vt_ref[8 * e:8 * e + 8, k, :] = v_ref[k, 8 * e:8 * e + 8, :]

    gt_ref[...] = jnp.zeros_like(gt_ref)
    first = me * n
    slot = lax.broadcasted_iota(jnp.int32, (J, wide), 0) + first
    lane = lax.broadcasted_iota(jnp.int32, (J, wide), 1)
    for k in range(K + 1):
        if k < K:
            c, v = cols_ref[k], vals_ref[k]
            v = jnp.where(lax.broadcasted_iota(jnp.int32, v.shape, 1) < P_SIZE, v, 0.0)
            hits = sum(jnp.where(c[b:b + 1] == slot, v[b:b + 1], 0.0) for b in range(c.shape[0]))
            rest = [sum(jnp.where(c[b:b + 1] == first + j, v[b:b + 1], 0.0) for b in range(c.shape[0]))
                    for j in range(J, n)]
        else:
            hits = jnp.where(lane == slot, 1.0, 0.0)
            rest = [jnp.where(lane[:1] == first + j, 1.0, 0.0) for j in range(J, n)]
        gt_ref[k * J:(k + 1) * J, 0:wide] = hits
        for j, r in enumerate(rest):
            at = (K + 1) * J + 16 * j + k
            gt_ref[at:at + 1, 0:wide] = r
    gt = gt_ref[...]
    lanes = lax.broadcasted_iota(jnp.int32, gt.shape, 1)
    total = gt.shape[1]
    step = (n + 7) // 8 * 8
    picked = jnp.zeros_like(gt)
    for p in range(P):
        at = ((p % 2) * (P // 2) + p // 2) * step
        shift = lax.rem(at - (me ^ p) * n + 8 * total, total)
        moved = pltpu.roll(gt, shift, 1)
        picked = jnp.where(jnp.logical_and(lanes >= at, lanes < at + n), moved, picked)
    g = jnp.transpose(picked)[:P * step]
    depth = g_ref.shape[2] // 3
    hi = g.astype(jnp.bfloat16)
    lo = (g - hi.astype(jnp.float32)).astype(jnp.bfloat16)
    M = P * step // 2
    for h in range(2):
        rows_h = slice(h * M, (h + 1) * M)
        g_ref[h] = jnp.concatenate([hi[rows_h, :depth], hi[rows_h, :depth], lo[rows_h, :depth]], 1)

    flat = source_ref.reshape(n * X * Y, Z)
    keep = jnp.where(lax.broadcasted_iota(jnp.int32, (n, Z), 0) + first < P_SIZE, 1.0, 0.0)

    def term(x, y):
        if not (0 <= x < X and 0 <= y < Y):
            return None
        w = (0.5 if x % 2 == 0 else 0.25) * (0.5 if y % 2 == 0 else 0.25)
        return flat[pl.ds(x * Y + y, n, stride=X * Y), :] * (w * keep)

    rs_ref[...] = jnp.zeros_like(rs_ref)
    B = Y // 2 + 2
    for (a, b), t in coarse_sums(X, Y, term).items():
        if t is not None:
            at = ((a + 1) * B + b + 1) * Z
            rs_ref[0:n, at:at + Z] = t


def prep(P, cols, vals, var, mean, source, xs, ys, after):
    n, X, Y, Z = source.shape
    K = var.shape[0]
    rows = X * Y + 2 * Y + 2 * X
    depth = (K + 1) * whole_groups(n) + 16 * (n - whole_groups(n))
    step = (n + 7) // 8 * 8
    wide = (X // 2 + 2) * (Y // 2 + 2) * Z
    return pl.pallas_call(
        functools.partial(prep_kernel, P, len(xs), len(ys)),
        out_shape=[jax.ShapeDtypeStruct((K + 1, rows, Z), jnp.float32),
                   jax.ShapeDtypeStruct((rows, 16, Z), jnp.float32),
                   jax.ShapeDtypeStruct((2, P * step // 2, 3 * depth), jnp.bfloat16),
                   jax.ShapeDtypeStruct((step, wide), jnp.float32)],
        in_specs=[VMEM] * (6 + len(xs) + len(ys)),
        out_specs=[VMEM] * 4,
        scratch_shapes=[pltpu.VMEM(((depth + 127) // 128 * 128, (P * step + 127) // 128 * 128), jnp.float32)],
        compiler_params=PARAMS,
        name="prep",
    )(cols, vals, var, mean, source, *xs, *ys, after)


def split(x):
    hi = x.astype(jnp.bfloat16)
    return hi, (x - hi.astype(jnp.float32)).astype(jnp.bfloat16)


def mxu(a, b):
    return jnp.dot(a, b, preferred_element_type=jnp.float32)


def sweep_kernel(nb, cols_ref, vals_ref, var_ref, mean_ref, source_ref, u_ref, v_ref, vt_ref, g_ref, rs_ref, *refs):
    blocks, refs = refs[:nb], refs[nb:]
    out_ref, send_ref, q_ref, full_ref, lap_ref, t_ref, z_ref = refs
    n, X, Y, Z = u_ref.shape
    K = var_ref.shape[0]
    me = lax.axis_index("chaos")
    fill_slots(me, blocks, full_ref)
    mean = mean_ref[...]
    inv = 1.0 / (9.0 * mean)

    def row(i, carry):
        acc = mixed_row(i, n, cols_ref, vals_ref, full_ref, var_ref)
        first = source_ref[i] - (mean * blocks[0][i] + acc)
        keep = jnp.where(me * n + i < P_SIZE, 1.0, 0.0)
        out_ref[i] = keep * (u_ref[i] + first * inv)
        return carry

    lax.fori_loop(0, n, row, 0)

    sub = lax.broadcasted_iota(jnp.int32, (Y, Z), 0)
    lane = lax.broadcasted_iota(jnp.int32, (Y, Z), 1)
    R = X * Y
    for s in range(n):
        plane = [out_ref[s, x] for x in range(X)]
        for x in range(X):
            v = plane[x]
            near = jnp.where(sub == 0, 0.0, pltpu.roll(v, 1, 0)) + jnp.where(sub == Y - 1, 0.0, pltpu.roll(v, Y - 1, 0))
            near += jnp.where(lane == 0, 0.0, pltpu.roll(v, 1, 1)) + jnp.where(lane == Z - 1, 0.0, pltpu.roll(v, Z - 1, 1))
            if x:
                near += plane[x - 1]
            if x + 1 < X:
                near += plane[x + 1]
            lap_ref[s * R + x * Y:s * R + (x + 1) * Y, :] = 6.0 * v - near
    at = row_list(X, Y)
    J = whole_groups(n)
    flat = out_ref.reshape(n * R, Z)

    def beside(x, y):
        inside = min(max(x, 0), X - 1) * Y + min(max(y, 0), Y - 1)
        return (lap_ref if (0 <= x < X and 0 <= y < Y) else flat), inside

    for (x, y), e in at.items():
        ref, r = beside(x, y)
        t_ref[e] = ref[pl.ds(r, J, stride=R), :]

    B = Y // 2 + 2

    def put(sums, where):
        for (a, b), q in sums.items():
            hi, lo = split(jnp.zeros((16, Z), jnp.float32) if q is None else q)
            c = ((a + 1) * B + b + 1) * Z
            q_ref[0, where, c:c + Z] = hi
            q_ref[1, where, c:c + Z] = lo

    def variable(k, carry):
        for g in range(J // 16):
            sums = coarse_sums(X, Y, lambda x, y: v_ref[k, pl.ds(at[x, y], 1), :] * t_ref[at[x, y], 16 * g:16 * g + 16, :])
            put(sums, pl.ds(pl.multiple_of(k * J + 16 * g, 16), 16))
        return carry

    lax.fori_loop(0, K + 1, variable, 0)
    for j in range(J, n):
        def term(x, y):
            ref, r = beside(x, y)
            return vt_ref[at[x, y]] * ref[j * R + r:j * R + r + 1, :]
        start = (K + 1) * J + 16 * (j - J)
        put(coarse_sums(X, Y, term), slice(start, start + 16))

    mix_rows(g_ref.at[1], q_ref, None, z_ref, send_ref, n)


def mix_rows(g_ref, q_ref, rs_ref, z_ref, out_ref, n):
    M = g_ref.shape[0]
    depth, wide = q_ref.shape[1], q_ref.shape[2]
    members, A, _, Z = out_ref.shape
    step = M // members
    c = lax.broadcasted_iota(jnp.int32, (2 * Z, Z), 1)
    z = lax.broadcasted_iota(jnp.int32, (2 * Z, Z), 0)
    half = Z // 2
    mid = jnp.where(c < half, 2 * c, Z + 2 * (c - half))
    same = (c < half) == (z < Z)
    weight = jnp.where(z == mid, 0.5, jnp.where(jnp.logical_and(same, jnp.abs(z - mid) == 1), 0.25, 0.0))
    weight = weight.astype(jnp.bfloat16)
    g_hi, g_lo = g_ref[:, :2 * depth], g_ref[:, 2 * depth:]
    chunks = wide // (2 * Z)
    for m in range(chunks):
        lanes = slice(2 * m * Z, 2 * (m + 1) * Z)
        high = q_ref[0, :, lanes]
        mixed = mxu(g_hi, jnp.concatenate([high, q_ref[1, :, lanes]], 0)) + mxu(g_lo, high)
        if rs_ref is not None:
            mixed = jnp.concatenate([mixed[:step] + rs_ref[:, lanes], mixed[step:]], 0)
        hi, lo = split(mixed)
        z_ref[m * M:(m + 1) * M, :2 * Z] = hi
        z_ref[m * M:(m + 1) * M, 2 * Z:] = lo
    weights = jnp.concatenate([weight, weight], 0)
    for m in range(chunks):
        part = mxu(z_ref[m * M:(m + 1) * M, :], weights)
        a, j = divmod(m, chunks // A)
        for p in range(members):
            out_ref[p, a, j * n:(j + 1) * n, :] = part[p * step:p * step + n]


def sweep(cols, vals, var, mean, source, u, tables, blocks):
    n, X, Y, Z = u.shape
    nb = len(blocks)
    v, vt, g, rs = tables
    rows = v.shape[1]
    part = jax.ShapeDtypeStruct((nb // 2, X // 2 + 2, (Y // 2 + 2) // 2 * n, Z), u.dtype)
    q = jax.ShapeDtypeStruct((2, g.shape[2] // 3, rs.shape[1]), jnp.bfloat16)
    z = pltpu.VMEM((rs.shape[1] // (2 * Z) * g.shape[1], 4 * Z), jnp.bfloat16)
    smoothed, send, q = pl.pallas_call(
        functools.partial(sweep_kernel, nb),
        out_shape=[jax.ShapeDtypeStruct(u.shape, u.dtype), part, q],
        in_specs=[SMEM, SMEM] + [VMEM] * (8 + nb),
        out_specs=[VMEM] * 3,
        scratch_shapes=[pltpu.VMEM((n * nb, X, Y, Z), jnp.float32),
                        pltpu.VMEM((n * X * Y, Z), jnp.float32),
                        pltpu.VMEM((rows, whole_groups(n), Z), jnp.float32),
                        z],
        compiler_params=PARAMS,
        name="sweep",
    )(cols, vals, var, mean, source, u, v, vt, g, rs, *blocks)

    def keep_kernel(g_ref, q_ref, rs_ref, out_ref, z_ref):
        mix_rows(g_ref.at[0], q_ref, rs_ref, z_ref, out_ref, n)

    keep = pl.pallas_call(
        keep_kernel,
        out_shape=part,
        in_specs=[VMEM] * 3,
        out_specs=VMEM,
        scratch_shapes=[z],
        compiler_params=PARAMS,
        name="keep",
    )(g, q, rs)
    return smoothed, keep, send


def final_kernel(ny, main_ref, *refs):
    ys, out_ref = refs[:ny], refs[ny]
    n, A, B, H = out_ref.shape
    fy = side_flags("gy")
    lane = lax.broadcasted_iota(jnp.int32, (n, 2 * H), 1)
    pairs = B // 2 + 1
    for a in range(A):
        low = sum(f[0] * r[a] for f, r in zip(fy, ys))
        high = sum(f[1] * r[a] for f, r in zip(fy, ys))
        part = [main_ref[a, m * n:(m + 1) * n, :] for m in range(pairs)]
        part[0] = part[0] + low
        part[-1] = part[-1] + high
        for b in range(B):
            v = part[(b + 1) // 2]
            if b % 2 == 0:
                v = pltpu.roll(v, H, 1)
            out_ref[:, a, b, :] = v[:, :H]


def final(main, ys, shape):
    return pl.pallas_call(
        functools.partial(final_kernel, len(ys)),
        out_shape=jax.ShapeDtypeStruct(shape, main.dtype),
        in_specs=[VMEM] * (1 + len(ys)),
        out_specs=VMEM,
        compiler_params=PARAMS,
        name="final",
    )(main, *ys)


def body(field, source, mean_coef, var_coefs, galerkin_cols, galerkin_vals):
    n, X, Y, Z = field.shape
    P = lax.axis_size("chaos")
    gx = lax.axis_size("gx")

    gy = lax.axis_size("gy")
    xs, ys = edges(field, var_coefs, mean_coef, phases(gx), phases(gy))
    xs = [lax.ppermute(v, "gx", pair_pairs(p, gx)) for p, v in enumerate(xs)]
    ys = [lax.ppermute(v, "gy", pair_pairs(p, gy)) for p, v in enumerate(ys)]
    lap = laplace(field, xs, ys)

    def beside():
        cols_all, vals_all, lap_now = lax.optimization_barrier((galerkin_cols, galerkin_vals, lap))
        first_row = lax.axis_index("chaos") * n
        cols = lax.dynamic_slice_in_dim(cols_all, first_row, n, 1).reshape(-1)
        vals = lax.dynamic_slice_in_dim(vals_all, first_row, n, 1).reshape(-1)
        tables = prep(P, jnp.transpose(cols_all, (0, 2, 1)), jnp.transpose(vals_all, (0, 2, 1)), var_coefs, mean_coef,
                      source, xs, ys, lap_now[:1, 0])
        return cols, vals, tables

    blocks, (cols, vals, tables) = gather_blocks(lap, beside)
    smoothed, keep, send = sweep(cols, vals, var_coefs, mean_coef, source, field, tables, blocks)

    parts = keep + lax.ppermute(send, "chaos", [(i, i ^ 1) for i in range(P)])
    main, edge_lo, edge_hi = parts[:, 1:-1], parts[:, 0], parts[:, -1]
    even = lax.axis_index("gx") % 2 == 0
    total = main[0]
    far = [(q, lax.ppermute(main[q], "chaos", [(i, i ^ (2 * q)) for i in range(P)])) for q in range(1, P // 2)]
    sides = []
    for p in range(phases(gx)):
        up = even if p == 0 else jnp.logical_not(even)
        edge = jnp.where(up, edge_hi, edge_lo)
        got = None
        for q in range(P // 2):
            pairs = [(i * P + j, partner(i, p, gx) * P + (j ^ (2 * q))) for i in range(gx) for j in range(P)]
            r = lax.ppermute(edge[q], ("gx", "chaos"), pairs)
            got = r if got is None else got + r
        sides.append(got)
    for q, r in far:
        total = total + r
    flags = side_flags("gx")
    low = sum(f[0] * r for f, r in zip(flags, sides))
    high = sum(f[1] * r for f, r in zip(flags, sides))
    A = total.shape[0]
    total = jnp.concatenate([total[:1] + low[None], total[1:]], 0)
    total = jnp.concatenate([total[:-1], total[-1:] + high[None]], 0)

    half = Z // 2
    lane = lax.broadcasted_iota(jnp.int32, (1, 1, Z), 2)
    low_rows = jnp.where(lane < half, total[:, :n], 0.0)
    high_rows = jnp.where(lane < half, 0.0, total[:, -n:])
    ys = swap_sides(low_rows, high_rows, "gy")
    coarse = final(total, ys, (n, A, Y // 2, half))
    return smoothed, coarse


def solution(mesh):
    return jax.shard_map(
        body,
        mesh=mesh,
        in_specs=(
            P("chaos", "gx", "gy", None),
            P("chaos", "gx", "gy", None),
            P("gx", "gy", None),
            P(None, "gx", "gy", None),
            P(),
            P(),
        ),
        out_specs=(P("chaos", "gx", "gy", None), P("chaos", "gx", "gy", None)),
        check_vma=False,
    )
```

```python
import functools

import jax
import jax.numpy as jnp
from jax import lax
from jax.experimental import pallas as pl
from jax.experimental.pallas import tpu as pltpu
from jax.sharding import PartitionSpec as P

P_SIZE = 66
PARAMS = pltpu.CompilerParams(vmem_limit_bytes=12 << 20)
VMEM = pl.BlockSpec(memory_space=pltpu.VMEM)
SMEM = pl.BlockSpec(memory_space=pltpu.SMEM)


def partner(i, phase, n):
    j = i + 1 if i % 2 == phase else i - 1
    return j if 0 <= j < n else i


def pair_pairs(phase, n):
    return [(i, partner(i, phase, n)) for i in range(n)]


def phases(n):
    return 1 if n == 2 else 2


def swap_sides(low, high, axis):
    n = lax.axis_size(axis)
    even = lax.axis_index(axis) % 2 == 0
    picks = [jnp.where(even, high, low), jnp.where(even, low, high)]
    return [lax.ppermute(picks[p], axis, pair_pairs(p, n)) for p in range(phases(n))]


def side_flags(axis):
    n = lax.axis_size(axis)
    i = lax.axis_index(axis)
    odd = lax.rem(i, 2)
    flags = []
    for p in range(phases(n)):
        up = jnp.logical_and(odd == p, i + 1 < n)
        down = jnp.logical_and(odd != p, i > 0)
        flags.append((jnp.where(down, 1.0, 0.0), jnp.where(up, 1.0, 0.0)))
    return flags


def edges_kernel(nx, ny, u_ref, var_ref, mean_ref, *refs):
    xs, ys = refs[:nx], refs[nx:]
    n, X, Y, Z = u_ref.shape
    K = var_ref.shape[0]
    even = [lax.rem(lax.axis_index(axis), 2) == 0 for axis in ("gx", "gy")]
    for p, ref in enumerate(xs):
        at = jnp.where(even[0] if p == 0 else jnp.logical_not(even[0]), X - 1, 0)
        for s in range(n):
            ref[s] = u_ref[s, at]
        for k in range(K):
            ref[n + k] = var_ref[k, at]
        ref[n + K] = mean_ref[at]
    flag = jnp.where(even[1], 1.0, 0.0)
    for src, where in ((u_ref, slice(0, n)), (var_ref, slice(n, n + K))):
        low, high = src[:, :, 0, :], src[:, :, Y - 1, :]
        for p, ref in enumerate(ys):
            f = flag if p == 0 else 1.0 - flag
            ref[where] = f * high + (1.0 - f) * low
    low, high = mean_ref[:, 0, :], mean_ref[:, Y - 1, :]
    for p, ref in enumerate(ys):
        f = flag if p == 0 else 1.0 - flag
        ref[n + K] = f * high + (1.0 - f) * low


def edges(u, var, mean, nx, ny):
    n, X, Y, Z = u.shape
    planes = n + var.shape[0] + 1
    out = [jax.ShapeDtypeStruct((planes, Y, Z), u.dtype)] * nx + [jax.ShapeDtypeStruct((planes, X, Z), u.dtype)] * ny
    res = pl.pallas_call(
        functools.partial(edges_kernel, nx, ny),
        out_shape=out,
        in_specs=[VMEM] * 3,
        out_specs=[VMEM] * len(out),
        compiler_params=PARAMS,
        name="edges",
    )(u, var, mean)
    return res[:nx], res[nx:]


def lap_kernel(nx, ny, u_ref, *refs):
    xs, ys, out_ref = refs[:nx], refs[nx:nx + ny], refs[nx + ny]
    n, X, Y, Z = u_ref.shape
    fx, fy = side_flags("gx"), side_flags("gy")
    sub = lax.broadcasted_iota(jnp.int32, (Y, Z), 0)
    lane = lax.broadcasted_iota(jnp.int32, (Y, Z), 1)
    for s in range(n):
        plane = [u_ref[s, x] for x in range(X)]
        below = sum(f[0] * r[s] for f, r in zip(fx, xs))
        above = sum(f[1] * r[s] for f, r in zip(fx, xs))
        row_lo = sum(f[0] * r[s] for f, r in zip(fy, ys))
        row_hi = sum(f[1] * r[s] for f, r in zip(fy, ys))
        for x in range(X):
            v = plane[x]
            near = (plane[x - 1] if x else below) + (plane[x + 1] if x + 1 < X else above)
            near += jnp.where(sub == 0, row_lo[x:x + 1], pltpu.roll(v, 1, 0))
            near += jnp.where(sub == Y - 1, row_hi[x:x + 1], pltpu.roll(v, Y - 1, 0))
            near += jnp.where(lane == 0, 0.0, pltpu.roll(v, 1, 1))
            near += jnp.where(lane == Z - 1, 0.0, pltpu.roll(v, Z - 1, 1))
            out_ref[s, x] = 6.0 * v - near


def laplace(u, xs, ys):
    return pl.pallas_call(
        functools.partial(lap_kernel, len(xs), len(ys)),
        out_shape=jax.ShapeDtypeStruct(u.shape, u.dtype),
        in_specs=[VMEM] * (1 + len(xs) + len(ys)),
        out_specs=VMEM,
        compiler_params=PARAMS,
        name="laplace",
    )(u, *xs, *ys)


def gather_blocks(own, beside):
    n = lax.axis_size("chaos")
    blocks = {0: own}
    d = n // 2
    extra = None
    while d:
        for p in list(blocks):
            block = blocks[p]
            if p and extra is None:
                extra = beside()
                block, extra = lax.optimization_barrier((block, extra))
            blocks[p ^ d] = lax.ppermute(block, "chaos", [(i, i ^ d) for i in range(n)])
        d //= 2
    return [blocks[p] for p in range(n)], extra


def fill_slots(me, blocks, full_ref):
    n = blocks[0].shape[0]
    for p, ref in enumerate(blocks):
        base = (me ^ p) * n
        for s in range(n):
            full_ref[base + s] = ref[s]


def mixed_row(i, n, cols_ref, vals_ref, full_ref, var_ref):
    K = var_ref.shape[0]
    nb = cols_ref.shape[0] // (K * n)
    acc = None
    for k in range(K):
        m = None
        for b in range(nb):
            at = (k * n + i) * nb + b
            t = vals_ref[at] * full_ref[cols_ref[at]]
            m = t if m is None else m + t
        m = var_ref[k] * m
        acc = m if acc is None else acc + m
    return acc


def row_list(X, Y):
    at = {(x, y): x * Y + y for x in range(X) for y in range(Y)}
    base = X * Y
    at.update({(-1, y): base + y for y in range(Y)})
    at.update({(X, y): base + Y + y for y in range(Y)})
    at.update({(x, -1): base + 2 * Y + x for x in range(X)})
    at.update({(x, Y): base + 2 * Y + X + x for x in range(X)})
    return at


def coarse_sums(X, Y, term):
    cols = {}
    for x in range(-1, X + 1):
        ys = [y for y in range(-1, Y + 1) if 0 <= x < X or 0 <= y < Y]
        got = {y: term(x, y) for y in ys}
        for b in range(-1, Y // 2 + 1):
            taps = [got[y] for y in (2 * b - 1, 2 * b, 2 * b + 1) if got.get(y) is not None]
            if taps:
                cols[x, b] = functools.reduce(jnp.add, taps)
    out = {}
    for a in range(-1, X // 2 + 1):
        for b in range(-1, Y // 2 + 1):
            taps = [cols[x, b] for x in (2 * a - 1, 2 * a, 2 * a + 1) if (x, b) in cols]
            out[a, b] = functools.reduce(jnp.add, taps) if taps else None
    return out


def whole_groups(n):
    return n // 16 * 16


def prep_kernel(P, nx, ny, cols_ref, vals_ref, var_ref, mean_ref, source_ref, u_ref, lap_ref, *refs):
    xs, ys = refs[:nx], refs[nx:nx + ny]
    v_ref, g_ref, rs_ref, base_ref, scaled_ref, gt_ref = refs[nx + ny:]
    n, X, Y, Z = source_ref.shape
    K = var_ref.shape[0]
    J = whole_groups(n)
    me = lax.axis_index("chaos")
    wide = cols_ref.shape[2]

    mean = mean_ref[...]
    inv = 1.0 / (9.0 * mean)
    for s in range(n):
        keep = jnp.where(me * n + s < P_SIZE, 1.0, 0.0)
        base_ref[s] = keep * (u_ref[s] + (source_ref[s] - mean * lap_ref[s]) * inv)
    for k in range(K):
        scaled_ref[k] = -inv * var_ref[k]

    fx, fy = side_flags("gx"), side_flags("gy")
    sub = lax.broadcasted_iota(jnp.int32, (Y, Z), 0)
    wy = jnp.where(lax.rem(sub, 2) == 0, 0.5, 0.25)
    base = X * Y
    for k in range(K + 1):
        for x in range(X):
            plane = var_ref[k, x] if k < K else mean_ref[x]
            v_ref[k, x * Y:(x + 1) * Y, :] = plane * (-(0.5 if x % 2 == 0 else 0.25) * wy)
        low = sum(f[0] * r[n + k] for f, r in zip(fx, xs))
        high = sum(f[1] * r[n + k] for f, r in zip(fx, xs))
        v_ref[k, base:base + Y, :] = low * (0.25 * wy)
        v_ref[k, base + Y:base + 2 * Y, :] = high * (0.5 * wy)
        low = sum(f[0] * r[n + k] for f, r in zip(fy, ys))
        high = sum(f[1] * r[n + k] for f, r in zip(fy, ys))
        wx = jnp.where(lax.rem(lax.broadcasted_iota(jnp.int32, (X, Z), 0), 2) == 0, 0.5, 0.25)
        v_ref[k, base + 2 * Y:base + 2 * Y + X, :] = low * (0.25 * wx)
        v_ref[k, base + 2 * Y + X:base + 2 * Y + 2 * X, :] = high * (0.5 * wx)

    gt_ref[...] = jnp.zeros_like(gt_ref)
    first = me * n
    slot = lax.broadcasted_iota(jnp.int32, (J, wide), 0) + first
    lane = lax.broadcasted_iota(jnp.int32, (J, wide), 1)
    for k in range(K + 1):
        if k < K:
            c, v = cols_ref[k], vals_ref[k]
            v = jnp.where(lax.broadcasted_iota(jnp.int32, v.shape, 1) < P_SIZE, v, 0.0)
            hits = sum(jnp.where(c[b:b + 1] == slot, v[b:b + 1], 0.0) for b in range(c.shape[0]))
            rest = [sum(jnp.where(c[b:b + 1] == first + j, v[b:b + 1], 0.0) for b in range(c.shape[0]))
                    for j in range(J, n)]
        else:
            hits = jnp.where(lane == slot, 1.0, 0.0)
            rest = [jnp.where(lane[:1] == first + j, 1.0, 0.0) for j in range(J, n)]
        gt_ref[k * J:(k + 1) * J, 0:wide] = hits
        for j, r in enumerate(rest):
            at = (K + 1) * J + 16 * j + k
            gt_ref[at:at + 1, 0:wide] = r
    gt = gt_ref[...]
    lanes = lax.broadcasted_iota(jnp.int32, gt.shape, 1)
    total = gt.shape[1]
    step = (n + 7) // 8 * 8
    picked = jnp.zeros_like(gt)
    for p in range(P):
        at = ((p % 2) * (P // 2) + p // 2) * step
        shift = lax.rem(at - (me ^ p) * n + 8 * total, total)
        moved = pltpu.roll(gt, shift, 1)
        picked = jnp.where(jnp.logical_and(lanes >= at, lanes < at + n), moved, picked)
    g = jnp.transpose(picked)[:P * step]
    depth = g_ref.shape[2] // 3
    hi = g.astype(jnp.bfloat16)
    lo = (g - hi.astype(jnp.float32)).astype(jnp.bfloat16)
    M = P * step // 2
    for h in range(2):
        rows_h = slice(h * M, (h + 1) * M)
        g_ref[h] = jnp.concatenate([hi[rows_h, :depth], hi[rows_h, :depth], lo[rows_h, :depth]], 1)

    flat = source_ref.reshape(n * X * Y, Z)
    keep = jnp.where(lax.broadcasted_iota(jnp.int32, (n, Z), 0) + first < P_SIZE, 1.0, 0.0)

    def term(x, y):
        if not (0 <= x < X and 0 <= y < Y):
            return None
        w = (0.5 if x % 2 == 0 else 0.25) * (0.5 if y % 2 == 0 else 0.25)
        return flat[pl.ds(x * Y + y, n, stride=X * Y), :] * (w * keep)

    rs_ref[...] = jnp.zeros_like(rs_ref)
    B = Y // 2 + 2
    for (a, b), t in coarse_sums(X, Y, term).items():
        if t is not None:
            at = ((a + 1) * B + b + 1) * Z
            rs_ref[0:n, at:at + Z] = t


def prep(P, cols, vals, var, mean, source, u, lap, xs, ys):
    n, X, Y, Z = source.shape
    K = var.shape[0]
    rows = X * Y + 2 * Y + 2 * X
    depth = (K + 1) * whole_groups(n) + 16 * (n - whole_groups(n))
    step = (n + 7) // 8 * 8
    wide = (X // 2 + 2) * (Y // 2 + 2) * Z
    return pl.pallas_call(
        functools.partial(prep_kernel, P, len(xs), len(ys)),
        out_shape=[jax.ShapeDtypeStruct((K + 1, rows, Z), jnp.float32),
                   jax.ShapeDtypeStruct((2, P * step // 2, 3 * depth), jnp.bfloat16),
                   jax.ShapeDtypeStruct((step, wide), jnp.float32),
                   jax.ShapeDtypeStruct(u.shape, jnp.float32),
                   jax.ShapeDtypeStruct(var.shape, jnp.float32)],
        in_specs=[VMEM] * (7 + len(xs) + len(ys)),
        out_specs=[VMEM] * 5,
        scratch_shapes=[pltpu.VMEM(((depth + 127) // 128 * 128, (P * step + 127) // 128 * 128), jnp.float32)],
        compiler_params=PARAMS,
        name="prep",
    )(cols, vals, var, mean, source, u, lap, *xs, *ys)


def split(x):
    hi = x.astype(jnp.bfloat16)
    return hi, (x - hi.astype(jnp.float32)).astype(jnp.bfloat16)


def mxu(a, b):
    return jnp.dot(a, b, preferred_element_type=jnp.float32)


def sweep_kernel(nb, cols_ref, vals_ref, base_ref, scaled_ref, v_ref, g_ref, *refs):
    blocks, refs = refs[:nb], refs[nb:]
    out_ref, send_ref, q_ref, full_ref, lap_ref, t_ref, z_ref = refs
    n, X, Y, Z = base_ref.shape
    K = scaled_ref.shape[0]
    me = lax.axis_index("chaos")
    fill_slots(me, blocks, full_ref)

    def row(i, carry):
        keep = jnp.where(me * n + i < P_SIZE, 1.0, 0.0)
        out_ref[i] = base_ref[i] + keep * mixed_row(i, n, cols_ref, vals_ref, full_ref, scaled_ref)
        return carry

    lax.fori_loop(0, n, row, 0)

    sub = lax.broadcasted_iota(jnp.int32, (Y, Z), 0)
    lane = lax.broadcasted_iota(jnp.int32, (Y, Z), 1)
    R = X * Y
    for s in range(n):
        plane = [out_ref[s, x] for x in range(X)]
        for x in range(X):
            v = plane[x]
            near = jnp.where(sub == 0, 0.0, pltpu.roll(v, 1, 0)) + jnp.where(sub == Y - 1, 0.0, pltpu.roll(v, Y - 1, 0))
            near += jnp.where(lane == 0, 0.0, pltpu.roll(v, 1, 1)) + jnp.where(lane == Z - 1, 0.0, pltpu.roll(v, Z - 1, 1))
            if x:
                near += plane[x - 1]
            if x + 1 < X:
                near += plane[x + 1]
            lap_ref[s * R + x * Y:s * R + (x + 1) * Y, :] = 6.0 * v - near
    at = row_list(X, Y)
    J = whole_groups(n)
    flat = out_ref.reshape(n * R, Z)

    def beside(x, y):
        inside = min(max(x, 0), X - 1) * Y + min(max(y, 0), Y - 1)
        return (lap_ref if (0 <= x < X and 0 <= y < Y) else flat), inside

    for (x, y), e in at.items():
        ref, r = beside(x, y)
        t_ref[e] = ref[pl.ds(r, J, stride=R), :]

    B = Y // 2 + 2

    def put(sums, where):
        for (a, b), q in sums.items():
            hi, lo = split(jnp.zeros((16, Z), jnp.float32) if q is None else q)
            c = ((a + 1) * B + b + 1) * Z
            q_ref[0, where, c:c + Z] = hi
            q_ref[1, where, c:c + Z] = lo

    def variable(k, carry):
        for g in range(J // 16):
            sums = coarse_sums(X, Y, lambda x, y: v_ref[k, pl.ds(at[x, y], 1), :] * t_ref[at[x, y], 16 * g:16 * g + 16, :])
            put(sums, pl.ds(pl.multiple_of(k * J + 16 * g, 16), 16))
        return carry

    lax.fori_loop(0, K + 1, variable, 0)
    flat_v = v_ref.reshape((K + 1) * v_ref.shape[1], Z)
    for j in range(J, n):
        def term(x, y):
            ref, r = beside(x, y)
            here = flat_v[pl.ds(at[x, y], K + 1, stride=v_ref.shape[1]), :]
            return jnp.concatenate([here, jnp.zeros((15 - K, Z), jnp.float32)], 0) * ref[j * R + r:j * R + r + 1, :]
        start = (K + 1) * J + 16 * (j - J)
        put(coarse_sums(X, Y, term), slice(start, start + 16))

    mix_rows(g_ref.at[1], q_ref, None, z_ref, send_ref, n)


def mix_rows(g_ref, q_ref, rs_ref, z_ref, out_ref, n):
    M = g_ref.shape[0]
    depth, wide = q_ref.shape[1], q_ref.shape[2]
    members, A, _, Z = out_ref.shape
    step = M // members
    c = lax.broadcasted_iota(jnp.int32, (2 * Z, Z), 1)
    z = lax.broadcasted_iota(jnp.int32, (2 * Z, Z), 0)
    half = Z // 2
    mid = jnp.where(c < half, 2 * c, Z + 2 * (c - half))
    same = (c < half) == (z < Z)
    weight = jnp.where(z == mid, 0.5, jnp.where(jnp.logical_and(same, jnp.abs(z - mid) == 1), 0.25, 0.0))
    weight = weight.astype(jnp.bfloat16)
    g_hi, g_lo = g_ref[:, :2 * depth], g_ref[:, 2 * depth:]
    chunks = wide // (2 * Z)
    for m in range(chunks):
        lanes = slice(2 * m * Z, 2 * (m + 1) * Z)
        high = q_ref[0, :, lanes]
        mixed = mxu(g_hi, jnp.concatenate([high, q_ref[1, :, lanes]], 0)) + mxu(g_lo, high)
        if rs_ref is not None:
            mixed = jnp.concatenate([mixed[:step] + rs_ref[:, lanes], mixed[step:]], 0)
        hi, lo = split(mixed)
        z_ref[m * M:(m + 1) * M, :2 * Z] = hi
        z_ref[m * M:(m + 1) * M, 2 * Z:] = lo
    weights = jnp.concatenate([weight, weight], 0)
    for m in range(chunks):
        part = mxu(z_ref[m * M:(m + 1) * M, :], weights)
        a, j = divmod(m, chunks // A)
        for p in range(members):
            out_ref[p, a, j * n:(j + 1) * n, :] = part[p * step:p * step + n]


def sweep(cols, vals, tables, blocks):
    n, X, Y, Z = blocks[0].shape
    nb = len(blocks)
    v, g, rs, base, scaled = tables
    u = base
    rows = v.shape[1]
    part = jax.ShapeDtypeStruct((nb // 2, X // 2 + 2, (Y // 2 + 2) // 2 * n, Z), u.dtype)
    q = jax.ShapeDtypeStruct((2, g.shape[2] // 3, rs.shape[1]), jnp.bfloat16)
    z = pltpu.VMEM((rs.shape[1] // (2 * Z) * g.shape[1], 4 * Z), jnp.bfloat16)
    smoothed, send, q = pl.pallas_call(
        functools.partial(sweep_kernel, nb),
        out_shape=[jax.ShapeDtypeStruct(u.shape, u.dtype), part, q],
        in_specs=[SMEM, SMEM] + [VMEM] * (4 + nb),
        out_specs=[VMEM] * 3,
        scratch_shapes=[pltpu.VMEM((n * nb, X, Y, Z), jnp.float32),
                        pltpu.VMEM((n * X * Y, Z), jnp.float32),
                        pltpu.VMEM((rows, whole_groups(n), Z), jnp.float32),
                        z],
        compiler_params=PARAMS,
        name="sweep",
    )(cols, vals, base, scaled, v, g, *blocks)

    def keep_kernel(g_ref, q_ref, rs_ref, out_ref, z_ref):
        mix_rows(g_ref.at[0], q_ref, rs_ref, z_ref, out_ref, n)

    keep = pl.pallas_call(
        keep_kernel,
        out_shape=part,
        in_specs=[VMEM] * 3,
        out_specs=VMEM,
        scratch_shapes=[z],
        compiler_params=PARAMS,
        name="keep",
    )(g, q, rs)
    return smoothed, keep, send


def final_kernel(ny, main_ref, *refs):
    ys, out_ref = refs[:ny], refs[ny]
    n, A, B, H = out_ref.shape
    fy = side_flags("gy")
    lane = lax.broadcasted_iota(jnp.int32, (n, 2 * H), 1)
    pairs = B // 2 + 1
    for a in range(A):
        low = sum(f[0] * r[a] for f, r in zip(fy, ys))
        high = sum(f[1] * r[a] for f, r in zip(fy, ys))
        part = [main_ref[a, m * n:(m + 1) * n, :] for m in range(pairs)]
        part[0] = part[0] + low
        part[-1] = part[-1] + high
        for b in range(B):
            v = part[(b + 1) // 2]
            if b % 2 == 0:
                v = pltpu.roll(v, H, 1)
            out_ref[:, a, b, :] = v[:, :H]


def final(main, ys, shape):
    return pl.pallas_call(
        functools.partial(final_kernel, len(ys)),
        out_shape=jax.ShapeDtypeStruct(shape, main.dtype),
        in_specs=[VMEM] * (1 + len(ys)),
        out_specs=VMEM,
        compiler_params=PARAMS,
        name="final",
    )(main, *ys)


def body(field, source, mean_coef, var_coefs, galerkin_cols, galerkin_vals):
    n, X, Y, Z = field.shape
    P = lax.axis_size("chaos")
    gx = lax.axis_size("gx")

    gy = lax.axis_size("gy")
    xs, ys = edges(field, var_coefs, mean_coef, phases(gx), phases(gy))
    xs = [lax.ppermute(v, "gx", pair_pairs(p, gx)) for p, v in enumerate(xs)]
    ys = [lax.ppermute(v, "gy", pair_pairs(p, gy)) for p, v in enumerate(ys)]
    lap = laplace(field, xs, ys)

    def beside():
        cols_all, vals_all, lap_now = galerkin_cols, galerkin_vals, lap
        first_row = lax.axis_index("chaos") * n
        cols = lax.dynamic_slice_in_dim(cols_all, first_row, n, 1).reshape(-1)
        vals = lax.dynamic_slice_in_dim(vals_all, first_row, n, 1).reshape(-1)
        tables = prep(P, jnp.transpose(cols_all, (0, 2, 1)), jnp.transpose(vals_all, (0, 2, 1)), var_coefs, mean_coef,
                      source, field, lap_now, xs, ys)
        return cols, vals, tables

    blocks, (cols, vals, tables) = gather_blocks(lap, beside)
    smoothed, keep, send = sweep(cols, vals, tables, blocks)

    parts = keep + lax.ppermute(send, "chaos", [(i, i ^ 1) for i in range(P)])
    main, edge_lo, edge_hi = parts[:, 1:-1], parts[:, 0], parts[:, -1]
    even = lax.axis_index("gx") % 2 == 0
    total = main[0]
    far = [(q, lax.ppermute(main[q], "chaos", [(i, i ^ (2 * q)) for i in range(P)])) for q in range(1, P // 2)]
    sides = []
    for p in range(phases(gx)):
        up = even if p == 0 else jnp.logical_not(even)
        edge = jnp.where(up, edge_hi, edge_lo)
        got = None
        for q in range(P // 2):
            pairs = [(i * P + j, partner(i, p, gx) * P + (j ^ (2 * q))) for i in range(gx) for j in range(P)]
            r = lax.ppermute(edge[q], ("gx", "chaos"), pairs)
            got = r if got is None else got + r
        sides.append(got)
    for q, r in far:
        total = total + r
    flags = side_flags("gx")
    low = sum(f[0] * r for f, r in zip(flags, sides))
    high = sum(f[1] * r for f, r in zip(flags, sides))
    A = total.shape[0]
    total = jnp.concatenate([total[:1] + low[None], total[1:]], 0)
    total = jnp.concatenate([total[:-1], total[-1:] + high[None]], 0)

    half = Z // 2
    lane = lax.broadcasted_iota(jnp.int32, (1, 1, Z), 2)
    low_rows = jnp.where(lane < half, total[:, :n], 0.0)
    high_rows = jnp.where(lane < half, 0.0, total[:, -n:])
    ys = swap_sides(low_rows, high_rows, "gy")
    coarse = final(total, ys, (n, A, Y // 2, half))
    return smoothed, coarse


def solution(mesh):
    return jax.shard_map(
        body,
        mesh=mesh,
        in_specs=(
            P("chaos", "gx", "gy", None),
            P("chaos", "gx", "gy", None),
            P("gx", "gy", None),
            P(None, "gx", "gy", None),
            P(),
            P(),
        ),
        out_specs=(P("chaos", "gx", "gy", None), P("chaos", "gx", "gy", None)),
        check_vma=False,
    )
```

```python
import functools

import jax
import jax.numpy as jnp
from jax import lax
from jax.experimental import pallas as pl
from jax.experimental.pallas import tpu as pltpu
from jax.sharding import PartitionSpec as P

P_SIZE = 66
PARAMS = pltpu.CompilerParams(vmem_limit_bytes=12 << 20)
VMEM = pl.BlockSpec(memory_space=pltpu.VMEM)
SMEM = pl.BlockSpec(memory_space=pltpu.SMEM)
HBM = pl.BlockSpec(memory_space=pltpu.HBM)


def partner(i, phase, n):
    j = i + 1 if i % 2 == phase else i - 1
    return j if 0 <= j < n else i


def pair_pairs(phase, n):
    return [(i, partner(i, phase, n)) for i in range(n)]


def phases(n):
    return 1 if n == 2 else 2


def swap_sides(low, high, axis):
    n = lax.axis_size(axis)
    even = lax.axis_index(axis) % 2 == 0
    picks = [jnp.where(even, high, low), jnp.where(even, low, high)]
    return [lax.ppermute(picks[p], axis, pair_pairs(p, n)) for p in range(phases(n))]


def side_flags(axis):
    n = lax.axis_size(axis)
    i = lax.axis_index(axis)
    odd = lax.rem(i, 2)
    flags = []
    for p in range(phases(n)):
        up = jnp.logical_and(odd == p, i + 1 < n)
        down = jnp.logical_and(odd != p, i > 0)
        flags.append((jnp.where(down, 1.0, 0.0), jnp.where(up, 1.0, 0.0)))
    return flags


def in_hbm(x):
    return pltpu.with_memory_space_constraint(x, pltpu.HBM)


def fetch(sem_ref, *pairs):
    copies = [pltpu.make_async_copy(a, b, sem_ref.at[i]) for i, (a, b) in enumerate(pairs)]
    for copy in copies:
        copy.start()
    for copy in copies:
        copy.wait()


def edges_kernel(nx, ny, u_hbm, var_hbm, mean_hbm, *refs):
    xs, ys = refs[:nx], refs[nx:nx + ny]
    u_ref, var_ref, mean_ref, sem_ref = refs[nx + ny:]
    fetch(sem_ref, (u_hbm, u_ref), (var_hbm, var_ref), (mean_hbm, mean_ref))
    n, X, Y, Z = u_ref.shape
    K = var_ref.shape[0]
    even = [lax.rem(lax.axis_index(axis), 2) == 0 for axis in ("gx", "gy")]
    for p, ref in enumerate(xs):
        at = jnp.where(even[0] if p == 0 else jnp.logical_not(even[0]), X - 1, 0)
        for s in range(n):
            ref[s] = u_ref[s, at]
        for k in range(K):
            ref[n + k] = var_ref[k, at]
        ref[n + K] = mean_ref[at]
    flag = jnp.where(even[1], 1.0, 0.0)
    for src, where in ((u_ref, slice(0, n)), (var_ref, slice(n, n + K))):
        low, high = src[:, :, 0, :], src[:, :, Y - 1, :]
        for p, ref in enumerate(ys):
            f = flag if p == 0 else 1.0 - flag
            ref[where] = f * high + (1.0 - f) * low
    low, high = mean_ref[:, 0, :], mean_ref[:, Y - 1, :]
    for p, ref in enumerate(ys):
        f = flag if p == 0 else 1.0 - flag
        ref[n + K] = f * high + (1.0 - f) * low


def edges(u, var, mean, nx, ny):
    n, X, Y, Z = u.shape
    planes = n + var.shape[0] + 1
    out = [jax.ShapeDtypeStruct((planes, Y, Z), u.dtype)] * nx + [jax.ShapeDtypeStruct((planes, X, Z), u.dtype)] * ny
    out.append(jax.ShapeDtypeStruct(u.shape, u.dtype))
    res = pl.pallas_call(
        functools.partial(edges_kernel, nx, ny),
        out_shape=out,
        in_specs=[HBM] * 3,
        out_specs=[VMEM] * len(out),
        scratch_shapes=[pltpu.VMEM(var.shape, var.dtype), pltpu.VMEM(mean.shape, mean.dtype),
                        pltpu.SemaphoreType.DMA((3,))],
        compiler_params=PARAMS,
        name="edges",
    )(*map(in_hbm, (u, var, mean)))
    return res[:nx], res[nx:nx + ny], res[nx + ny]


def lap_kernel(nx, ny, u_ref, *refs):
    xs, ys, out_ref = refs[:nx], refs[nx:nx + ny], refs[nx + ny]
    n, X, Y, Z = u_ref.shape
    fx, fy = side_flags("gx"), side_flags("gy")
    sub = lax.broadcasted_iota(jnp.int32, (Y, Z), 0)
    lane = lax.broadcasted_iota(jnp.int32, (Y, Z), 1)
    for s in range(n):
        plane = [u_ref[s, x] for x in range(X)]
        below = sum(f[0] * r[s] for f, r in zip(fx, xs))
        above = sum(f[1] * r[s] for f, r in zip(fx, xs))
        row_lo = sum(f[0] * r[s] for f, r in zip(fy, ys))
        row_hi = sum(f[1] * r[s] for f, r in zip(fy, ys))
        for x in range(X):
            v = plane[x]
            near = (plane[x - 1] if x else below) + (plane[x + 1] if x + 1 < X else above)
            near += jnp.where(sub == 0, row_lo[x:x + 1], pltpu.roll(v, 1, 0))
            near += jnp.where(sub == Y - 1, row_hi[x:x + 1], pltpu.roll(v, Y - 1, 0))
            near += jnp.where(lane == 0, 0.0, pltpu.roll(v, 1, 1))
            near += jnp.where(lane == Z - 1, 0.0, pltpu.roll(v, Z - 1, 1))
            out_ref[s, x] = 6.0 * v - near


def laplace(u, xs, ys):
    return pl.pallas_call(
        functools.partial(lap_kernel, len(xs), len(ys)),
        out_shape=jax.ShapeDtypeStruct(u.shape, u.dtype),
        in_specs=[VMEM] * (1 + len(xs) + len(ys)),
        out_specs=VMEM,
        compiler_params=PARAMS,
        name="laplace",
    )(u, *xs, *ys)


def gather_blocks(own, beside):
    n = lax.axis_size("chaos")
    blocks = {0: own}
    d = n // 2
    extra = None
    while d:
        for p in list(blocks):
            block = blocks[p]
            if p and extra is None:
                extra = beside()
                block, extra = lax.optimization_barrier((block, extra))
            blocks[p ^ d] = lax.ppermute(block, "chaos", [(i, i ^ d) for i in range(n)])
        d //= 2
    return [blocks[p] for p in range(n)], extra


def fill_slots(me, blocks, full_ref):
    n = blocks[0].shape[0]
    for p, ref in enumerate(blocks):
        base = (me ^ p) * n
        for s in range(n):
            full_ref[base + s] = ref[s]


def mixed_row(i, n, cols_ref, vals_ref, full_ref, var_ref):
    K = var_ref.shape[0]
    nb = cols_ref.shape[0] // (K * n)
    acc = None
    for k in range(K):
        m = None
        for b in range(nb):
            at = (k * n + i) * nb + b
            t = vals_ref[at] * full_ref[cols_ref[at]]
            m = t if m is None else m + t
        m = var_ref[k] * m
        acc = m if acc is None else acc + m
    return acc


def row_list(X, Y):
    at = {(x, y): x * Y + y for x in range(X) for y in range(Y)}
    base = X * Y
    at.update({(-1, y): base + y for y in range(Y)})
    at.update({(X, y): base + Y + y for y in range(Y)})
    at.update({(x, -1): base + 2 * Y + x for x in range(X)})
    at.update({(x, Y): base + 2 * Y + X + x for x in range(X)})
    return at


def coarse_sums(X, Y, term):
    cols = {}
    for x in range(-1, X + 1):
        ys = [y for y in range(-1, Y + 1) if 0 <= x < X or 0 <= y < Y]
        got = {y: term(x, y) for y in ys}
        for b in range(-1, Y // 2 + 1):
            taps = [got[y] for y in (2 * b - 1, 2 * b, 2 * b + 1) if got.get(y) is not None]
            if taps:
                cols[x, b] = functools.reduce(jnp.add, taps)
    out = {}
    for a in range(-1, X // 2 + 1):
        for b in range(-1, Y // 2 + 1):
            taps = [cols[x, b] for x in (2 * a - 1, 2 * a, 2 * a + 1) if (x, b) in cols]
            out[a, b] = functools.reduce(jnp.add, taps) if taps else None
    return out


def whole_groups(n):
    return n // 16 * 16


def prep_kernel(P, nx, ny, cols_hbm, vals_hbm, var_hbm, mean_hbm, source_hbm, u_ref, lap_ref, *refs):
    xs, ys = refs[:nx], refs[nx:nx + ny]
    v_ref, g_ref, rs_ref, base_ref, scaled_ref, gt_ref, cols_ref, vals_ref, var_ref, mean_ref, source_ref, sem_ref = refs[nx + ny:]
    fetch(sem_ref, (source_hbm, source_ref), (var_hbm, var_ref), (mean_hbm, mean_ref), (cols_hbm, cols_ref),
          (vals_hbm, vals_ref))
    n, X, Y, Z = source_ref.shape
    K = var_ref.shape[0]
    J = whole_groups(n)
    me = lax.axis_index("chaos")
    wide = cols_ref.shape[2]

    mean = mean_ref[...]
    inv = 1.0 / (9.0 * mean)
    for s in range(n):
        keep = jnp.where(me * n + s < P_SIZE, 1.0, 0.0)
        base_ref[s] = keep * (u_ref[s] + (source_ref[s] - mean * lap_ref[s]) * inv)
    for k in range(K):
        scaled_ref[k] = -inv * var_ref[k]

    fx, fy = side_flags("gx"), side_flags("gy")
    sub = lax.broadcasted_iota(jnp.int32, (Y, Z), 0)
    wy = jnp.where(lax.rem(sub, 2) == 0, 0.5, 0.25)
    base = X * Y
    for k in range(K + 1):
        for x in range(X):
            plane = var_ref[k, x] if k < K else mean_ref[x]
            v_ref[k, x * Y:(x + 1) * Y, :] = plane * (-(0.5 if x % 2 == 0 else 0.25) * wy)
        low = sum(f[0] * r[n + k] for f, r in zip(fx, xs))
        high = sum(f[1] * r[n + k] for f, r in zip(fx, xs))
        v_ref[k, base:base + Y, :] = low * (0.25 * wy)
        v_ref[k, base + Y:base + 2 * Y, :] = high * (0.5 * wy)
        low = sum(f[0] * r[n + k] for f, r in zip(fy, ys))
        high = sum(f[1] * r[n + k] for f, r in zip(fy, ys))
        wx = jnp.where(lax.rem(lax.broadcasted_iota(jnp.int32, (X, Z), 0), 2) == 0, 0.5, 0.25)
        v_ref[k, base + 2 * Y:base + 2 * Y + X, :] = low * (0.25 * wx)
        v_ref[k, base + 2 * Y + X:base + 2 * Y + 2 * X, :] = high * (0.5 * wx)

    gt_ref[...] = jnp.zeros_like(gt_ref)
    first = me * n
    slot = lax.broadcasted_iota(jnp.int32, (J, wide), 0) + first
    lane = lax.broadcasted_iota(jnp.int32, (J, wide), 1)
    for k in range(K + 1):
        if k < K:
            c, v = cols_ref[k], vals_ref[k]
            v = jnp.where(lax.broadcasted_iota(jnp.int32, v.shape, 1) < P_SIZE, v, 0.0)
            hits = sum(jnp.where(c[b:b + 1] == slot, v[b:b + 1], 0.0) for b in range(c.shape[0]))
            rest = [sum(jnp.where(c[b:b + 1] == first + j, v[b:b + 1], 0.0) for b in range(c.shape[0]))
                    for j in range(J, n)]
        else:
            hits = jnp.where(lane == slot, 1.0, 0.0)
            rest = [jnp.where(lane[:1] == first + j, 1.0, 0.0) for j in range(J, n)]
        gt_ref[k * J:(k + 1) * J, 0:wide] = hits
        for j, r in enumerate(rest):
            at = (K + 1) * J + 16 * j + k
            gt_ref[at:at + 1, 0:wide] = r
    gt = gt_ref[...]
    lanes = lax.broadcasted_iota(jnp.int32, gt.shape, 1)
    total = gt.shape[1]
    step = (n + 7) // 8 * 8
    picked = jnp.zeros_like(gt)
    for p in range(P):
        at = ((p % 2) * (P // 2) + p // 2) * step
        shift = lax.rem(at - (me ^ p) * n + 8 * total, total)
        moved = pltpu.roll(gt, shift, 1)
        picked = jnp.where(jnp.logical_and(lanes >= at, lanes < at + n), moved, picked)
    g = jnp.transpose(picked)[:P * step]
    depth = g_ref.shape[2] // 3
    hi = g.astype(jnp.bfloat16)
    lo = (g - hi.astype(jnp.float32)).astype(jnp.bfloat16)
    M = P * step // 2
    for h in range(2):
        rows_h = slice(h * M, (h + 1) * M)
        g_ref[h] = jnp.concatenate([hi[rows_h, :depth], hi[rows_h, :depth], lo[rows_h, :depth]], 1)

    flat = source_ref.reshape(n * X * Y, Z)
    keep = jnp.where(lax.broadcasted_iota(jnp.int32, (n, Z), 0) + first < P_SIZE, 1.0, 0.0)

    def term(x, y):
        if not (0 <= x < X and 0 <= y < Y):
            return None
        w = (0.5 if x % 2 == 0 else 0.25) * (0.5 if y % 2 == 0 else 0.25)
        return flat[pl.ds(x * Y + y, n, stride=X * Y), :] * (w * keep)

    rs_ref[...] = jnp.zeros_like(rs_ref)
    B = Y // 2 + 2
    for (a, b), t in coarse_sums(X, Y, term).items():
        if t is not None:
            at = ((a + 1) * B + b + 1) * Z
            rs_ref[0:n, at:at + Z] = t


def prep(P, cols, vals, var, mean, source, u, lap, xs, ys):
    n, X, Y, Z = source.shape
    K = var.shape[0]
    rows = X * Y + 2 * Y + 2 * X
    depth = (K + 1) * whole_groups(n) + 16 * (n - whole_groups(n))
    step = (n + 7) // 8 * 8
    wide = (X // 2 + 2) * (Y // 2 + 2) * Z
    return pl.pallas_call(
        functools.partial(prep_kernel, P, len(xs), len(ys)),
        out_shape=[jax.ShapeDtypeStruct((K + 1, rows, Z), jnp.float32),
                   jax.ShapeDtypeStruct((2, P * step // 2, 3 * depth), jnp.bfloat16),
                   jax.ShapeDtypeStruct((step, wide), jnp.float32),
                   jax.ShapeDtypeStruct(u.shape, jnp.float32),
                   jax.ShapeDtypeStruct(var.shape, jnp.float32)],
        in_specs=[HBM] * 5 + [VMEM] * (2 + len(xs) + len(ys)),
        out_specs=[VMEM] * 5,
        scratch_shapes=[pltpu.VMEM(((depth + 127) // 128 * 128, (P * step + 127) // 128 * 128), jnp.float32)]
        + [pltpu.VMEM(a.shape, a.dtype) for a in (cols, vals, var, mean, source)] + [pltpu.SemaphoreType.DMA((5,))],
        compiler_params=PARAMS,
        name="prep",
    )(*map(in_hbm, (cols, vals, var, mean, source)), u, lap, *xs, *ys)


def split(x):
    hi = x.astype(jnp.bfloat16)
    return hi, (x - hi.astype(jnp.float32)).astype(jnp.bfloat16)


def mxu(a, b):
    return jnp.dot(a, b, preferred_element_type=jnp.float32)


def sweep_kernel(nb, cols_ref, vals_ref, base_ref, scaled_ref, v_ref, g_ref, *refs):
    blocks, refs = refs[:nb], refs[nb:]
    out_ref, send_ref, q_ref, full_ref, lap_ref, t_ref, z_ref = refs
    n, X, Y, Z = base_ref.shape
    K = scaled_ref.shape[0]
    me = lax.axis_index("chaos")
    fill_slots(me, blocks, full_ref)

    def row(i, carry):
        keep = jnp.where(me * n + i < P_SIZE, 1.0, 0.0)
        out_ref[i] = base_ref[i] + keep * mixed_row(i, n, cols_ref, vals_ref, full_ref, scaled_ref)
        return carry

    lax.fori_loop(0, n, row, 0)

    sub = lax.broadcasted_iota(jnp.int32, (Y, Z), 0)
    lane = lax.broadcasted_iota(jnp.int32, (Y, Z), 1)
    R = X * Y
    for s in range(n):
        plane = [out_ref[s, x] for x in range(X)]
        for x in range(X):
            v = plane[x]
            near = jnp.where(sub == 0, 0.0, pltpu.roll(v, 1, 0)) + jnp.where(sub == Y - 1, 0.0, pltpu.roll(v, Y - 1, 0))
            near += jnp.where(lane == 0, 0.0, pltpu.roll(v, 1, 1)) + jnp.where(lane == Z - 1, 0.0, pltpu.roll(v, Z - 1, 1))
            if x:
                near += plane[x - 1]
            if x + 1 < X:
                near += plane[x + 1]
            lap_ref[s * R + x * Y:s * R + (x + 1) * Y, :] = 6.0 * v - near
    at = row_list(X, Y)
    J = whole_groups(n)
    flat = out_ref.reshape(n * R, Z)

    def beside(x, y):
        inside = min(max(x, 0), X - 1) * Y + min(max(y, 0), Y - 1)
        return (lap_ref if (0 <= x < X and 0 <= y < Y) else flat), inside

    for (x, y), e in at.items():
        ref, r = beside(x, y)
        t_ref[e] = ref[pl.ds(r, J, stride=R), :]

    B = Y // 2 + 2

    def put(sums, where):
        for (a, b), q in sums.items():
            hi, lo = split(jnp.zeros((16, Z), jnp.float32) if q is None else q)
            c = ((a + 1) * B + b + 1) * Z
            q_ref[0, where, c:c + Z] = hi
            q_ref[1, where, c:c + Z] = lo

    def variable(k, carry):
        for g in range(J // 16):
            sums = coarse_sums(X, Y, lambda x, y: v_ref[k, pl.ds(at[x, y], 1), :] * t_ref[at[x, y], 16 * g:16 * g + 16, :])
            put(sums, pl.ds(pl.multiple_of(k * J + 16 * g, 16), 16))
        return carry

    lax.fori_loop(0, K + 1, variable, 0)
    flat_v = v_ref.reshape((K + 1) * v_ref.shape[1], Z)
    for j in range(J, n):
        def term(x, y):
            ref, r = beside(x, y)
            here = flat_v[pl.ds(at[x, y], K + 1, stride=v_ref.shape[1]), :]
            return jnp.concatenate([here, jnp.zeros((15 - K, Z), jnp.float32)], 0) * ref[j * R + r:j * R + r + 1, :]
        start = (K + 1) * J + 16 * (j - J)
        put(coarse_sums(X, Y, term), slice(start, start + 16))

    mix_rows(g_ref.at[1], q_ref, None, z_ref, send_ref, n)


def mix_rows(g_ref, q_ref, rs_ref, z_ref, out_ref, n):
    M = g_ref.shape[0]
    depth, wide = q_ref.shape[1], q_ref.shape[2]
    members, A, _, Z = out_ref.shape
    step = M // members
    c = lax.broadcasted_iota(jnp.int32, (2 * Z, Z), 1)
    z = lax.broadcasted_iota(jnp.int32, (2 * Z, Z), 0)
    half = Z // 2
    mid = jnp.where(c < half, 2 * c, Z + 2 * (c - half))
    same = (c < half) == (z < Z)
    weight = jnp.where(z == mid, 0.5, jnp.where(jnp.logical_and(same, jnp.abs(z - mid) == 1), 0.25, 0.0))
    weight = weight.astype(jnp.bfloat16)
    g_hi, g_lo = g_ref[:, :2 * depth], g_ref[:, 2 * depth:]
    chunks = wide // (2 * Z)
    for m in range(chunks):
        lanes = slice(2 * m * Z, 2 * (m + 1) * Z)
        high = q_ref[0, :, lanes]
        mixed = mxu(g_hi, jnp.concatenate([high, q_ref[1, :, lanes]], 0)) + mxu(g_lo, high)
        if rs_ref is not None:
            mixed = jnp.concatenate([mixed[:step] + rs_ref[:, lanes], mixed[step:]], 0)
        hi, lo = split(mixed)
        z_ref[m * M:(m + 1) * M, :2 * Z] = hi
        z_ref[m * M:(m + 1) * M, 2 * Z:] = lo
    weights = jnp.concatenate([weight, weight], 0)
    for m in range(chunks):
        part = mxu(z_ref[m * M:(m + 1) * M, :], weights)
        a, j = divmod(m, chunks // A)
        for p in range(members):
            out_ref[p, a, j * n:(j + 1) * n, :] = part[p * step:p * step + n]


def sweep(cols, vals, tables, blocks):
    n, X, Y, Z = blocks[0].shape
    nb = len(blocks)
    v, g, rs, base, scaled = tables
    u = base
    rows = v.shape[1]
    part = jax.ShapeDtypeStruct((nb // 2, X // 2 + 2, (Y // 2 + 2) // 2 * n, Z), u.dtype)
    q = jax.ShapeDtypeStruct((2, g.shape[2] // 3, rs.shape[1]), jnp.bfloat16)
    z = pltpu.VMEM((rs.shape[1] // (2 * Z) * g.shape[1], 4 * Z), jnp.bfloat16)
    smoothed, send, q = pl.pallas_call(
        functools.partial(sweep_kernel, nb),
        out_shape=[jax.ShapeDtypeStruct(u.shape, u.dtype), part, q],
        in_specs=[SMEM, SMEM] + [VMEM] * (4 + nb),
        out_specs=[VMEM] * 3,
        scratch_shapes=[pltpu.VMEM((n * nb, X, Y, Z), jnp.float32),
                        pltpu.VMEM((n * X * Y, Z), jnp.float32),
                        pltpu.VMEM((rows, whole_groups(n), Z), jnp.float32),
                        z],
        compiler_params=PARAMS,
        name="sweep",
    )(cols, vals, base, scaled, v, g, *blocks)

    def keep_kernel(g_ref, q_ref, rs_ref, out_ref, z_ref):
        mix_rows(g_ref.at[0], q_ref, rs_ref, z_ref, out_ref, n)

    keep = pl.pallas_call(
        keep_kernel,
        out_shape=part,
        in_specs=[VMEM] * 3,
        out_specs=VMEM,
        scratch_shapes=[z],
        compiler_params=PARAMS,
        name="keep",
    )(g, q, rs)
    return smoothed, keep, send


def final_kernel(ny, main_ref, *refs):
    ys, out_ref = refs[:ny], refs[ny]
    n, A, B, H = out_ref.shape
    fy = side_flags("gy")
    lane = lax.broadcasted_iota(jnp.int32, (n, 2 * H), 1)
    pairs = B // 2 + 1
    for a in range(A):
        low = sum(f[0] * r[a] for f, r in zip(fy, ys))
        high = sum(f[1] * r[a] for f, r in zip(fy, ys))
        part = [main_ref[a, m * n:(m + 1) * n, :] for m in range(pairs)]
        part[0] = part[0] + low
        part[-1] = part[-1] + high
        for b in range(B):
            v = part[(b + 1) // 2]
            if b % 2 == 0:
                v = pltpu.roll(v, H, 1)
            out_ref[:, a, b, :] = v[:, :H]


def final(main, ys, shape):
    return pl.pallas_call(
        functools.partial(final_kernel, len(ys)),
        out_shape=jax.ShapeDtypeStruct(shape, main.dtype),
        in_specs=[VMEM] * (1 + len(ys)),
        out_specs=VMEM,
        compiler_params=PARAMS,
        name="final",
    )(main, *ys)


def body(field, source, mean_coef, var_coefs, galerkin_cols, galerkin_vals):
    n, X, Y, Z = field.shape
    P = lax.axis_size("chaos")
    gx = lax.axis_size("gx")

    gy = lax.axis_size("gy")
    xs, ys, u = edges(field, var_coefs, mean_coef, phases(gx), phases(gy))
    xs = [lax.ppermute(v, "gx", pair_pairs(p, gx)) for p, v in enumerate(xs)]
    ys = [lax.ppermute(v, "gy", pair_pairs(p, gy)) for p, v in enumerate(ys)]
    lap = laplace(u, xs, ys)

    def beside():
        cols_all, vals_all, lap_now = galerkin_cols, galerkin_vals, lap
        first_row = lax.axis_index("chaos") * n
        cols = lax.dynamic_slice_in_dim(cols_all, first_row, n, 1).reshape(-1)
        vals = lax.dynamic_slice_in_dim(vals_all, first_row, n, 1).reshape(-1)
        tables = prep(P, jnp.transpose(cols_all, (0, 2, 1)), jnp.transpose(vals_all, (0, 2, 1)), var_coefs, mean_coef,
                      source, u, lap_now, xs, ys)
        return cols, vals, tables

    blocks, (cols, vals, tables) = gather_blocks(lap, beside)
    smoothed, keep, send = sweep(cols, vals, tables, blocks)

    parts = keep + lax.ppermute(send, "chaos", [(i, i ^ 1) for i in range(P)])
    main, edge_lo, edge_hi = parts[:, 1:-1], parts[:, 0], parts[:, -1]
    even = lax.axis_index("gx") % 2 == 0
    total = main[0]
    far = [(q, lax.ppermute(main[q], "chaos", [(i, i ^ (2 * q)) for i in range(P)])) for q in range(1, P // 2)]
    sides = []
    for p in range(phases(gx)):
        up = even if p == 0 else jnp.logical_not(even)
        edge = jnp.where(up, edge_hi, edge_lo)
        got = None
        for q in range(P // 2):
            pairs = [(i * P + j, partner(i, p, gx) * P + (j ^ (2 * q))) for i in range(gx) for j in range(P)]
            r = lax.ppermute(edge[q], ("gx", "chaos"), pairs)
            got = r if got is None else got + r
        sides.append(got)
    for q, r in far:
        total = total + r
    flags = side_flags("gx")
    low = sum(f[0] * r for f, r in zip(flags, sides))
    high = sum(f[1] * r for f, r in zip(flags, sides))
    A = total.shape[0]
    total = jnp.concatenate([total[:1] + low[None], total[1:]], 0)
    total = jnp.concatenate([total[:-1], total[-1:] + high[None]], 0)

    half = Z // 2
    lane = lax.broadcasted_iota(jnp.int32, (1, 1, Z), 2)
    low_rows = jnp.where(lane < half, total[:, :n], 0.0)
    high_rows = jnp.where(lane < half, 0.0, total[:, -n:])
    ys = swap_sides(low_rows, high_rows, "gy")
    coarse = final(total, ys, (n, A, Y // 2, half))
    return smoothed, coarse


def solution(mesh):
    return jax.shard_map(
        body,
        mesh=mesh,
        in_specs=(
            P("chaos", "gx", "gy", None),
            P("chaos", "gx", "gy", None),
            P("gx", "gy", None),
            P(None, "gx", "gy", None),
            P(),
            P(),
        ),
        out_specs=(P("chaos", "gx", "gy", None), P("chaos", "gx", "gy", None)),
        check_vma=False,
    )
```

```python
import functools

import jax
import jax.numpy as jnp
from jax import lax
from jax.experimental import pallas as pl
from jax.experimental.pallas import tpu as pltpu
from jax.sharding import PartitionSpec as P

P_SIZE = 66
PARAMS = pltpu.CompilerParams(vmem_limit_bytes=12 << 20)
VMEM = pl.BlockSpec(memory_space=pltpu.VMEM)
HBM = pl.BlockSpec(memory_space=pltpu.HBM)


def partner(i, phase, n):
    j = i + 1 if i % 2 == phase else i - 1
    return j if 0 <= j < n else i


def pair_pairs(phase, n):
    return [(i, partner(i, phase, n)) for i in range(n)]


def phases(n):
    return 1 if n == 2 else 2


def swap_sides(low, high, axis):
    n = lax.axis_size(axis)
    even = lax.axis_index(axis) % 2 == 0
    picks = [jnp.where(even, high, low), jnp.where(even, low, high)]
    return [lax.ppermute(picks[p], axis, pair_pairs(p, n)) for p in range(phases(n))]


def side_flags(axis):
    n = lax.axis_size(axis)
    i = lax.axis_index(axis)
    odd = lax.rem(i, 2)
    flags = []
    for p in range(phases(n)):
        up = jnp.logical_and(odd == p, i + 1 < n)
        down = jnp.logical_and(odd != p, i > 0)
        flags.append((jnp.where(down, 1.0, 0.0), jnp.where(up, 1.0, 0.0)))
    return flags


def in_hbm(x):
    return pltpu.with_memory_space_constraint(x, pltpu.HBM)


def fetch(sem_ref, *pairs):
    copies = [pltpu.make_async_copy(a, b, sem_ref.at[i]) for i, (a, b) in enumerate(pairs)]
    for copy in copies:
        copy.start()
    for copy in copies:
        copy.wait()


def edges_kernel(nx, ny, u_hbm, var_hbm, mean_hbm, *refs):
    xs, ys = refs[:nx], refs[nx:nx + ny]
    u_ref, var_ref, mean_ref, sem_ref = refs[nx + ny:]
    fetch(sem_ref, (u_hbm, u_ref), (var_hbm, var_ref), (mean_hbm, mean_ref))
    n, X, Y, Z = u_ref.shape
    K = var_ref.shape[0]
    even = [lax.rem(lax.axis_index(axis), 2) == 0 for axis in ("gx", "gy")]
    for p, ref in enumerate(xs):
        at = jnp.where(even[0] if p == 0 else jnp.logical_not(even[0]), X - 1, 0)
        for s in range(n):
            ref[s] = u_ref[s, at]
        for k in range(K):
            ref[n + k] = var_ref[k, at]
        ref[n + K] = mean_ref[at]
    flag = jnp.where(even[1], 1.0, 0.0)
    for src, where in ((u_ref, slice(0, n)), (var_ref, slice(n, n + K))):
        low, high = src[:, :, 0, :], src[:, :, Y - 1, :]
        for p, ref in enumerate(ys):
            f = flag if p == 0 else 1.0 - flag
            ref[where] = f * high + (1.0 - f) * low
    low, high = mean_ref[:, 0, :], mean_ref[:, Y - 1, :]
    for p, ref in enumerate(ys):
        f = flag if p == 0 else 1.0 - flag
        ref[n + K] = f * high + (1.0 - f) * low


def edges(u, var, mean, nx, ny):
    n, X, Y, Z = u.shape
    planes = n + var.shape[0] + 1
    out = [jax.ShapeDtypeStruct((planes, Y, Z), u.dtype)] * nx + [jax.ShapeDtypeStruct((planes, X, Z), u.dtype)] * ny
    out.append(jax.ShapeDtypeStruct(u.shape, u.dtype))
    res = pl.pallas_call(
        functools.partial(edges_kernel, nx, ny),
        out_shape=out,
        in_specs=[HBM] * 3,
        out_specs=[VMEM] * len(out),
        scratch_shapes=[pltpu.VMEM(var.shape, var.dtype), pltpu.VMEM(mean.shape, mean.dtype),
                        pltpu.SemaphoreType.DMA((3,))],
        compiler_params=PARAMS,
        name="edges",
    )(*map(in_hbm, (u, var, mean)))
    return res[:nx], res[nx:nx + ny], res[nx + ny]


def lap_kernel(nx, ny, u_ref, *refs):
    xs, ys, out_ref = refs[:nx], refs[nx:nx + ny], refs[nx + ny]
    n, X, Y, Z = u_ref.shape
    fx, fy = side_flags("gx"), side_flags("gy")
    sub = lax.broadcasted_iota(jnp.int32, (Y, Z), 0)
    lane = lax.broadcasted_iota(jnp.int32, (Y, Z), 1)
    for s in range(n):
        plane = [u_ref[s, x] for x in range(X)]
        below = sum(f[0] * r[s] for f, r in zip(fx, xs))
        above = sum(f[1] * r[s] for f, r in zip(fx, xs))
        row_lo = sum(f[0] * r[s] for f, r in zip(fy, ys))
        row_hi = sum(f[1] * r[s] for f, r in zip(fy, ys))
        for x in range(X):
            v = plane[x]
            near = (plane[x - 1] if x else below) + (plane[x + 1] if x + 1 < X else above)
            near += jnp.where(sub == 0, row_lo[x:x + 1], pltpu.roll(v, 1, 0))
            near += jnp.where(sub == Y - 1, row_hi[x:x + 1], pltpu.roll(v, Y - 1, 0))
            near += jnp.where(lane == 0, 0.0, pltpu.roll(v, 1, 1))
            near += jnp.where(lane == Z - 1, 0.0, pltpu.roll(v, Z - 1, 1))
            out_ref[s, x] = 6.0 * v - near


def laplace(u, xs, ys):
    return pl.pallas_call(
        functools.partial(lap_kernel, len(xs), len(ys)),
        out_shape=jax.ShapeDtypeStruct(u.shape, u.dtype),
        in_specs=[VMEM] * (1 + len(xs) + len(ys)),
        out_specs=VMEM,
        compiler_params=PARAMS,
        name="laplace",
    )(u, *xs, *ys)


def gather_blocks(own, beside):
    n = lax.axis_size("chaos")
    blocks = {0: own}
    d = n // 2
    extra = None
    while d:
        for p in list(blocks):
            block = blocks[p]
            if p and extra is None:
                extra = beside()
                block, extra = lax.optimization_barrier((block, extra))
            blocks[p ^ d] = lax.ppermute(block, "chaos", [(i, i ^ d) for i in range(n)])
        d //= 2
    return [blocks[p] for p in range(n)], extra


def row_list(X, Y):
    at = {(x, y): x * Y + y for x in range(X) for y in range(Y)}
    base = X * Y
    at.update({(-1, y): base + y for y in range(Y)})
    at.update({(X, y): base + Y + y for y in range(Y)})
    at.update({(x, -1): base + 2 * Y + x for x in range(X)})
    at.update({(x, Y): base + 2 * Y + X + x for x in range(X)})
    return at


def coarse_sums(X, Y, term):
    cols = {}
    for x in range(-1, X + 1):
        ys = [y for y in range(-1, Y + 1) if 0 <= x < X or 0 <= y < Y]
        got = {y: term(x, y) for y in ys}
        for b in range(-1, Y // 2 + 1):
            taps = [got[y] for y in (2 * b - 1, 2 * b, 2 * b + 1) if got.get(y) is not None]
            if taps:
                cols[x, b] = functools.reduce(jnp.add, taps)
    out = {}
    for a in range(-1, X // 2 + 1):
        for b in range(-1, Y // 2 + 1):
            taps = [cols[x, b] for x in (2 * a - 1, 2 * a, 2 * a + 1) if (x, b) in cols]
            out[a, b] = functools.reduce(jnp.add, taps) if taps else None
    return out


def whole_groups(n):
    return n // 16 * 16


def prep_kernel(P, nx, ny, cols_hbm, vals_hbm, var_hbm, mean_hbm, source_hbm, u_ref, lap_ref, *refs):
    xs, ys = refs[:nx], refs[nx:nx + ny]
    v_ref, g_ref, rs_ref, base_ref, scaled_ref, first_ref, weight_ref = refs[nx + ny:nx + ny + 7]
    gt_ref, pad_c_ref, pad_v_ref, cols_ref, vals_ref, var_ref, mean_ref, source_ref, sem_ref = refs[nx + ny + 7:]
    fetch(sem_ref, (source_hbm, source_ref), (var_hbm, var_ref), (mean_hbm, mean_ref), (cols_hbm, cols_ref),
          (vals_hbm, vals_ref))
    n, X, Y, Z = source_ref.shape
    K = var_ref.shape[0]
    J = whole_groups(n)
    me = lax.axis_index("chaos")
    wide = cols_ref.shape[2]

    mean = mean_ref[...]
    inv = 1.0 / (9.0 * mean)
    for s in range(n):
        keep = jnp.where(me * n + s < P_SIZE, 1.0, 0.0)
        base_ref[s] = keep * (u_ref[s] + (source_ref[s] - mean * lap_ref[s]) * inv)
    for k in range(K):
        scaled_ref[k] = -inv * var_ref[k]

    J, nb, wide = whole_groups(n), cols_ref.shape[1], cols_ref.shape[2]
    for k in range(K):
        pad_c_ref[k, :, 0:wide] = cols_ref[k]
        pad_v_ref[k, :, 0:wide] = vals_ref[k]
    M1, D1 = first_ref.shape[0], first_ref.shape[1] // 3
    tiles = (M1 + 127) // 128
    own = lax.broadcasted_iota(jnp.int32, (nb, 128), 1)
    c_tile = [jnp.full((nb, 128), -1, jnp.int32)] * tiles
    v_tile = [jnp.zeros((nb, 128), jnp.float32)] * tiles
    for k in range(K):
        c, v = pad_c_ref[k], pad_v_ref[k]
        v = jnp.where(own < P_SIZE, v, 0.0)
        spans = [(k * J + 16 * g, 16 * g, 16) for g in range(J // 16)]
        spans += [(K * J + 16 * (j - J) + k, j, 1) for j in range(J, n)]
        for at, slot, count in spans:
            t, lane_at = divmod(at, 128)
            shift = lax.rem(lane_at - (me * n + slot) + 8 * 128, 128)
            here = jnp.logical_and(own >= lane_at, own < lane_at + count)
            c_tile[t] = jnp.where(here, pltpu.roll(c, shift, 1), c_tile[t])
            v_tile[t] = jnp.where(here, pltpu.roll(v, shift, 1), v_tile[t])
    row_id = lax.broadcasted_iota(jnp.int32, (128, 128), 0)
    slot_id = jnp.full((128, 128), -2, jnp.int32)
    for p in range(P):
        whole = jnp.logical_and(row_id >= p * J, row_id < (p + 1) * J)
        slot_id = jnp.where(whole, (me ^ p) * n + row_id - p * J, slot_id)
        for j in range(J, n):
            slot_id = jnp.where(row_id == P * J + p * (n - J) + j - J, (me ^ p) * n + j, slot_id)
    for t in range(tiles):
        hits = sum(jnp.where(c_tile[t][b:b + 1] == slot_id, v_tile[t][b:b + 1], 0.0) for b in range(nb))
        hi, lo = split(jnp.transpose(hits))
        count = min(128, M1 - t * 128)
        first_ref[t * 128:t * 128 + count, :] = jnp.concatenate(
            [hi[:count, :D1], lo[:count, :D1], hi[:count, :D1]], 1)

    c = lax.broadcasted_iota(jnp.int32, (2 * Z, Z), 1)
    z = lax.broadcasted_iota(jnp.int32, (2 * Z, Z), 0)
    half = Z // 2
    mid = jnp.where(c < half, 2 * c, Z + 2 * (c - half))
    same = (c < half) == (z < Z)
    weight = jnp.where(z == mid, 0.5, jnp.where(jnp.logical_and(same, jnp.abs(z - mid) == 1), 0.25, 0.0))
    weight = weight.astype(jnp.bfloat16)
    weight_ref[...] = jnp.concatenate([weight, weight], 0)

    fx, fy = side_flags("gx"), side_flags("gy")
    sub = lax.broadcasted_iota(jnp.int32, (Y, Z), 0)
    wy = jnp.where(lax.rem(sub, 2) == 0, 0.5, 0.25)
    base = X * Y
    for k in range(K + 1):
        for x in range(X):
            plane = var_ref[k, x] if k < K else mean_ref[x]
            v_ref[k, x * Y:(x + 1) * Y, :] = plane * (-(0.5 if x % 2 == 0 else 0.25) * wy)
        low = sum(f[0] * r[n + k] for f, r in zip(fx, xs))
        high = sum(f[1] * r[n + k] for f, r in zip(fx, xs))
        v_ref[k, base:base + Y, :] = low * (0.25 * wy)
        v_ref[k, base + Y:base + 2 * Y, :] = high * (0.5 * wy)
        low = sum(f[0] * r[n + k] for f, r in zip(fy, ys))
        high = sum(f[1] * r[n + k] for f, r in zip(fy, ys))
        wx = jnp.where(lax.rem(lax.broadcasted_iota(jnp.int32, (X, Z), 0), 2) == 0, 0.5, 0.25)
        v_ref[k, base + 2 * Y:base + 2 * Y + X, :] = low * (0.25 * wx)
        v_ref[k, base + 2 * Y + X:base + 2 * Y + 2 * X, :] = high * (0.5 * wx)

    gt_ref[...] = jnp.zeros_like(gt_ref)
    first = me * n
    slot = lax.broadcasted_iota(jnp.int32, (J, wide), 0) + first
    lane = lax.broadcasted_iota(jnp.int32, (J, wide), 1)
    for k in range(K + 1):
        if k < K:
            c, v = cols_ref[k], vals_ref[k]
            v = jnp.where(lax.broadcasted_iota(jnp.int32, v.shape, 1) < P_SIZE, v, 0.0)
            hits = sum(jnp.where(c[b:b + 1] == slot, v[b:b + 1], 0.0) for b in range(c.shape[0]))
            rest = [sum(jnp.where(c[b:b + 1] == first + j, v[b:b + 1], 0.0) for b in range(c.shape[0]))
                    for j in range(J, n)]
        else:
            hits = jnp.where(lane == slot, 1.0, 0.0)
            rest = [jnp.where(lane[:1] == first + j, 1.0, 0.0) for j in range(J, n)]
        gt_ref[k * J:(k + 1) * J, 0:wide] = hits
        for j, r in enumerate(rest):
            at = (K + 1) * J + 16 * j + k
            gt_ref[at:at + 1, 0:wide] = r
    gt = gt_ref[...]
    lanes = lax.broadcasted_iota(jnp.int32, gt.shape, 1)
    total = gt.shape[1]
    step = (n + 7) // 8 * 8
    picked = jnp.zeros_like(gt)
    for p in range(P):
        at = ((p % 2) * (P // 2) + p // 2) * step
        shift = lax.rem(at - (me ^ p) * n + 8 * total, total)
        moved = pltpu.roll(gt, shift, 1)
        picked = jnp.where(jnp.logical_and(lanes >= at, lanes < at + n), moved, picked)
    g = jnp.transpose(picked)[:P * step]
    depth = g_ref.shape[2] // 3
    hi = g.astype(jnp.bfloat16)
    lo = (g - hi.astype(jnp.float32)).astype(jnp.bfloat16)
    M = P * step // 2
    for h in range(2):
        rows_h = slice(h * M, (h + 1) * M)
        g_ref[h] = jnp.concatenate([hi[rows_h, :depth], hi[rows_h, :depth], lo[rows_h, :depth]], 1)

    flat = source_ref.reshape(n * X * Y, Z)
    keep = jnp.where(lax.broadcasted_iota(jnp.int32, (n, Z), 0) + first < P_SIZE, 1.0, 0.0)

    def term(x, y):
        if not (0 <= x < X and 0 <= y < Y):
            return None
        w = (0.5 if x % 2 == 0 else 0.25) * (0.5 if y % 2 == 0 else 0.25)
        return flat[pl.ds(x * Y + y, n, stride=X * Y), :] * (w * keep)

    rs_ref[...] = jnp.zeros_like(rs_ref)
    B = Y // 2 + 2
    for (a, b), t in coarse_sums(X, Y, term).items():
        if t is not None:
            at = ((a + 1) * B + b + 1) * Z
            rs_ref[0:n, at:at + Z] = t


def prep(P, cols, vals, var, mean, source, u, lap, xs, ys):
    n, X, Y, Z = source.shape
    K = var.shape[0]
    rows = X * Y + 2 * Y + 2 * X
    depth = (K + 1) * whole_groups(n) + 16 * (n - whole_groups(n))
    step = (n + 7) // 8 * 8
    wide = (X // 2 + 2) * (Y // 2 + 2) * Z
    return pl.pallas_call(
        functools.partial(prep_kernel, P, len(xs), len(ys)),
        out_shape=[jax.ShapeDtypeStruct((K + 1, rows, Z), jnp.float32),
                   jax.ShapeDtypeStruct((2, P * step // 2, 3 * depth), jnp.bfloat16),
                   jax.ShapeDtypeStruct((step, wide), jnp.float32),
                   jax.ShapeDtypeStruct(u.shape, jnp.float32),
                   jax.ShapeDtypeStruct(var.shape, jnp.float32),
                   jax.ShapeDtypeStruct((K * whole_groups(n) + 16 * (n - whole_groups(n)),
                                         3 * (P * whole_groups(n) + 16)), jnp.bfloat16),
                   jax.ShapeDtypeStruct((4 * Z, Z), jnp.bfloat16)],
        in_specs=[HBM] * 5 + [VMEM] * (2 + len(xs) + len(ys)),
        out_specs=[VMEM] * 7,
        scratch_shapes=[pltpu.VMEM(((depth + 127) // 128 * 128, (P * step + 127) // 128 * 128), jnp.float32),
                        pltpu.VMEM(cols.shape[:2] + (128,), cols.dtype), pltpu.VMEM(cols.shape[:2] + (128,), vals.dtype)]
        + [pltpu.VMEM(a.shape, a.dtype) for a in (cols, vals, var, mean, source)] + [pltpu.SemaphoreType.DMA((5,))],
        compiler_params=PARAMS,
        name="prep",
    )(*map(in_hbm, (cols, vals, var, mean, source)), u, lap, *xs, *ys)


def split(x):
    hi = x.astype(jnp.bfloat16)
    return hi, (x - hi.astype(jnp.float32)).astype(jnp.bfloat16)


def mxu(a, b):
    return jnp.dot(a, b, preferred_element_type=jnp.float32)


def side_by_side(blocks, first, hi_ref, lo_ref, rest_ref):
    n, X, Y, Z = blocks[0].shape
    R, J = X * Y, whole_groups(n)
    rest_ref[...] = jnp.zeros_like(rest_ref)
    for p, ref in enumerate(blocks):
        rows = ref.reshape(n * R, Z)
        for r in range(R):
            hi, lo = split(rows[pl.ds(r, J, stride=R), :])
            hi_ref[p * J:(p + 1) * J, r * Z:(r + 1) * Z] = hi
            lo_ref[p * J:(p + 1) * J, r * Z:(r + 1) * Z] = lo
        for j in range(J, n):
            for r in range(0, R, 8):
                at = 16 * r + (first + p) * (n - J) + j - J
                rest_ref[pl.ds(at, 8, stride=16), :] = rows[j * R + r:j * R + r + 8, :]


def early(blocks):
    n, X, Y, Z = blocks[0].shape
    rows = len(blocks) * whole_groups(n)

    def kernel(*refs):
        side_by_side(refs[:len(blocks)], 0, *refs[len(blocks):])

    return pl.pallas_call(
        kernel,
        out_shape=[jax.ShapeDtypeStruct((rows, X * Y * Z), jnp.bfloat16)] * 2
        + [jax.ShapeDtypeStruct((16 * X * Y, Z), jnp.float32)],
        in_specs=[VMEM] * len(blocks),
        out_specs=[VMEM] * 3,
        compiler_params=PARAMS,
        name="early",
    )(*blocks)


def sweep_kernel(nb, base_ref, scaled_ref, v_ref, first_ref, g_ref, weight_ref, ehi_ref, elo_ref, erest_ref, *refs):
    blocks, refs = refs[:1], refs[1:]
    out_ref, send_ref, q_ref, lhi_ref, llo_ref, rest_ref, prod_ref, s_ref, t_ref, lap_ref, z_ref = refs
    n, X, Y, Z = base_ref.shape
    K = scaled_ref.shape[0]
    R, J = X * Y, whole_groups(n)

    side_by_side(blocks, nb - 1, lhi_ref, llo_ref, rest_ref)
    for r in range(R):
        hi, lo = split(rest_ref[16 * r:16 * r + 16, :] + erest_ref[16 * r:16 * r + 16, :])
        lhi_ref[J:J + 16, r * Z:(r + 1) * Z] = hi
        llo_ref[J:J + 16, r * Z:(r + 1) * Z] = lo

    first = first_ref[...]
    base = base_ref.reshape(n * R, Z)
    scaled = scaled_ref.reshape(K * R, Z)
    out = out_ref.reshape(n * R, Z)
    for e in range(0, R, 2):
        lanes = slice(e * Z, (e + 2) * Z)
        high = jnp.concatenate([ehi_ref[:, lanes], lhi_ref[:, lanes]], 0)
        both = mxu(first, jnp.concatenate([high, high, elo_ref[:, lanes], llo_ref[:, lanes]], 0))
        for r in (e, e + 1):
            mixed = both[:, (r - e) * Z:(r - e + 1) * Z]
            acc = base[pl.ds(r, J, stride=R), :]
            for k in range(K):
                acc = acc + scaled[k * R + r:k * R + r + 1, :] * mixed[k * J:(k + 1) * J]
            s_ref[r] = acc
            out[pl.ds(r, J, stride=R), :] = acc
            for j in range(J, n):
                at = K * J + 16 * (j - J)
                prod_ref[((j - J) * R + r) * 16:((j - J) * R + r) * 16 + K, :] = (
                    scaled[pl.ds(r, K, stride=R), :] * mixed[at:at + K])
    for j in range(J, n):
        acc = base[j * R:(j + 1) * R, :]
        for k in range(K):
            acc = acc + prod_ref[pl.ds((j - J) * R * 16 + k, R, stride=16), :]
        out[j * R:(j + 1) * R, :] = acc

    wide = lax.broadcasted_iota(jnp.int32, (J, Z), 1)
    for x in range(X):
        for y in range(Y):
            v = s_ref[x * Y + y]
            near = jnp.where(wide == 0, 0.0, pltpu.roll(v, 1, 1)) + jnp.where(wide == Z - 1, 0.0, pltpu.roll(v, Z - 1, 1))
            for x2, y2 in ((x - 1, y), (x + 1, y), (x, y - 1), (x, y + 1)):
                if 0 <= x2 < X and 0 <= y2 < Y:
                    near = near + s_ref[x2 * Y + y2]
            t_ref[x * Y + y] = 6.0 * v - near
    sub = lax.broadcasted_iota(jnp.int32, (Y, Z), 0)
    lane = lax.broadcasted_iota(jnp.int32, (Y, Z), 1)
    for s in range(J, n):
        plane = [out_ref[s, x] for x in range(X)]
        for x in range(X):
            v = plane[x]
            near = jnp.where(sub == 0, 0.0, pltpu.roll(v, 1, 0)) + jnp.where(sub == Y - 1, 0.0, pltpu.roll(v, Y - 1, 0))
            near += jnp.where(lane == 0, 0.0, pltpu.roll(v, 1, 1)) + jnp.where(lane == Z - 1, 0.0, pltpu.roll(v, Z - 1, 1))
            if x:
                near += plane[x - 1]
            if x + 1 < X:
                near += plane[x + 1]
            lap_ref[(s - J) * R + x * Y:(s - J) * R + (x + 1) * Y, :] = 6.0 * v - near
    at = row_list(X, Y)

    def inside(x, y):
        return min(max(x, 0), X - 1) * Y + min(max(y, 0), Y - 1)

    def own(x, y):
        return 0 <= x < X and 0 <= y < Y

    B = Y // 2 + 2

    def put(sums, where):
        for (a, b), q in sums.items():
            hi, lo = split(jnp.zeros((16, Z), jnp.float32) if q is None else q)
            c = ((a + 1) * B + b + 1) * Z
            q_ref[0, where, c:c + Z] = hi
            q_ref[1, where, c:c + Z] = lo

    def variable(k, carry):
        for g in range(J // 16):
            def term(x, y):
                ref = t_ref if own(x, y) else s_ref
                return v_ref[k, pl.ds(at[x, y], 1), :] * ref[inside(x, y), 16 * g:16 * g + 16, :]
            sums = coarse_sums(X, Y, term)
            put(sums, pl.ds(pl.multiple_of(k * J + 16 * g, 16), 16))
        return carry

    lax.fori_loop(0, K + 1, variable, 0)
    flat_v = v_ref.reshape((K + 1) * v_ref.shape[1], Z)
    for j in range(J, n):
        def term(x, y):
            ref, r = (lap_ref, (j - J) * R) if own(x, y) else (out, j * R)
            r = r + inside(x, y)
            here = flat_v[pl.ds(at[x, y], K + 1, stride=v_ref.shape[1]), :]
            return jnp.concatenate([here, jnp.zeros((15 - K, Z), jnp.float32)], 0) * ref[r:r + 1, :]
        start = (K + 1) * J + 16 * (j - J)
        put(coarse_sums(X, Y, term), slice(start, start + 16))

    mix_rows(g_ref.at[1], q_ref, None, weight_ref, z_ref, send_ref, n)


def mix_rows(g_ref, q_ref, rs_ref, weight_ref, z_ref, out_ref, n):
    M = g_ref.shape[0]
    depth, wide = q_ref.shape[1], q_ref.shape[2]
    members, A, _, Z = out_ref.shape
    step = M // members
    g_hi, g_lo = g_ref[:, :2 * depth], g_ref[:, 2 * depth:]
    chunks = wide // (2 * Z)
    for m in range(chunks):
        lanes = slice(2 * m * Z, 2 * (m + 1) * Z)
        high = q_ref[0, :, lanes]
        mixed = mxu(g_hi, jnp.concatenate([high, q_ref[1, :, lanes]], 0)) + mxu(g_lo, high)
        if rs_ref is not None:
            mixed = jnp.concatenate([mixed[:step] + rs_ref[:, lanes], mixed[step:]], 0)
        hi, lo = split(mixed)
        z_ref[m * M:(m + 1) * M, :2 * Z] = hi
        z_ref[m * M:(m + 1) * M, 2 * Z:] = lo
    weights = weight_ref[...]
    for m in range(chunks):
        part = mxu(z_ref[m * M:(m + 1) * M, :], weights)
        a, j = divmod(m, chunks // A)
        for p in range(members):
            out_ref[p, a, j * n:(j + 1) * n, :] = part[p * step:p * step + n]


def sweep(tables, early_parts, blocks):
    n, X, Y, Z = blocks[0].shape
    nb = len(blocks)
    v, g, rs, base, scaled, first, weight = tables
    u = base
    rows = v.shape[1]
    part = jax.ShapeDtypeStruct((nb // 2, X // 2 + 2, (Y // 2 + 2) // 2 * n, Z), u.dtype)
    q = jax.ShapeDtypeStruct((2, g.shape[2] // 3, rs.shape[1]), jnp.bfloat16)
    z = pltpu.VMEM((rs.shape[1] // (2 * Z) * g.shape[1], 4 * Z), jnp.bfloat16)
    smoothed, send, q = pl.pallas_call(
        functools.partial(sweep_kernel, nb),
        out_shape=[jax.ShapeDtypeStruct(u.shape, u.dtype), part, q],
        in_specs=[VMEM] * 10,
        out_specs=[VMEM] * 3,
        scratch_shapes=[pltpu.VMEM((whole_groups(n) + 16, X * Y * Z), jnp.bfloat16),
                        pltpu.VMEM((whole_groups(n) + 16, X * Y * Z), jnp.bfloat16),
                        pltpu.VMEM((16 * X * Y, Z), jnp.float32),
                        pltpu.VMEM(((n - whole_groups(n)) * X * Y * 16, Z), jnp.float32),
                        pltpu.VMEM((X * Y, whole_groups(n), Z), jnp.float32),
                        pltpu.VMEM((X * Y, whole_groups(n), Z), jnp.float32),
                        pltpu.VMEM(((n - whole_groups(n)) * X * Y, Z), jnp.float32),
                        z],
        compiler_params=PARAMS,
        name="sweep",
    )(base, scaled, v, first, g, weight, *early_parts, blocks[-1])

    def keep_kernel(g_ref, q_ref, rs_ref, weight_ref, out_ref, z_ref):
        mix_rows(g_ref.at[0], q_ref, rs_ref, weight_ref, z_ref, out_ref, n)

    keep = pl.pallas_call(
        keep_kernel,
        out_shape=part,
        in_specs=[VMEM] * 4,
        out_specs=VMEM,
        scratch_shapes=[z],
        compiler_params=PARAMS,
        name="keep",
    )(g, q, rs, weight)
    return smoothed, keep, send


def final_kernel(ny, main_ref, *refs):
    ys, out_ref = refs[:ny], refs[ny]
    n, A, B, H = out_ref.shape
    fy = side_flags("gy")
    lane = lax.broadcasted_iota(jnp.int32, (n, 2 * H), 1)
    pairs = B // 2 + 1
    for a in range(A):
        low = sum(f[0] * r[a] for f, r in zip(fy, ys))
        high = sum(f[1] * r[a] for f, r in zip(fy, ys))
        part = [main_ref[a, m * n:(m + 1) * n, :] for m in range(pairs)]
        part[0] = part[0] + low
        part[-1] = part[-1] + high
        for b in range(B):
            v = part[(b + 1) // 2]
            if b % 2 == 0:
                v = pltpu.roll(v, H, 1)
            out_ref[:, a, b, :] = v[:, :H]


def final(main, ys, shape):
    return pl.pallas_call(
        functools.partial(final_kernel, len(ys)),
        out_shape=jax.ShapeDtypeStruct(shape, main.dtype),
        in_specs=[VMEM] * (1 + len(ys)),
        out_specs=VMEM,
        compiler_params=PARAMS,
        name="final",
    )(main, *ys)


def body(field, source, mean_coef, var_coefs, galerkin_cols, galerkin_vals):
    n, X, Y, Z = field.shape
    P = lax.axis_size("chaos")
    gx = lax.axis_size("gx")

    gy = lax.axis_size("gy")
    xs, ys, u = edges(field, var_coefs, mean_coef, phases(gx), phases(gy))
    xs = [lax.ppermute(v, "gx", pair_pairs(p, gx)) for p, v in enumerate(xs)]
    ys = [lax.ppermute(v, "gy", pair_pairs(p, gy)) for p, v in enumerate(ys)]
    lap = laplace(u, xs, ys)

    def beside():
        return prep(P, jnp.transpose(galerkin_cols, (0, 2, 1)), jnp.transpose(galerkin_vals, (0, 2, 1)), var_coefs,
                    mean_coef, source, u, lap, xs, ys)

    blocks, tables = gather_blocks(lap, beside)
    smoothed, keep, send = sweep(tables, early(blocks[:-1]), blocks)

    parts = keep + lax.ppermute(send, "chaos", [(i, i ^ 1) for i in range(P)])
    main, edge_lo, edge_hi = parts[:, 1:-1], parts[:, 0], parts[:, -1]
    even = lax.axis_index("gx") % 2 == 0
    total = main[0]
    far = [(q, lax.ppermute(main[q], "chaos", [(i, i ^ (2 * q)) for i in range(P)])) for q in range(1, P // 2)]
    sides = []
    for p in range(phases(gx)):
        up = even if p == 0 else jnp.logical_not(even)
        edge = jnp.where(up, edge_hi, edge_lo)
        got = None
        for q in range(P // 2):
            pairs = [(i * P + j, partner(i, p, gx) * P + (j ^ (2 * q))) for i in range(gx) for j in range(P)]
            r = lax.ppermute(edge[q], ("gx", "chaos"), pairs)
            got = r if got is None else got + r
        sides.append(got)
    for q, r in far:
        total = total + r
    flags = side_flags("gx")
    low = sum(f[0] * r for f, r in zip(flags, sides))
    high = sum(f[1] * r for f, r in zip(flags, sides))
    A = total.shape[0]
    total = jnp.concatenate([total[:1] + low[None], total[1:]], 0)
    total = jnp.concatenate([total[:-1], total[-1:] + high[None]], 0)

    half = Z // 2
    lane = lax.broadcasted_iota(jnp.int32, (1, 1, Z), 2)
    low_rows = jnp.where(lane < half, total[:, :n], 0.0)
    high_rows = jnp.where(lane < half, 0.0, total[:, -n:])
    ys = swap_sides(low_rows, high_rows, "gy")
    coarse = final(total, ys, (n, A, Y // 2, half))
    return smoothed, coarse


def solution(mesh):
    return jax.shard_map(
        body,
        mesh=mesh,
        in_specs=(
            P("chaos", "gx", "gy", None),
            P("chaos", "gx", "gy", None),
            P("gx", "gy", None),
            P(None, "gx", "gy", None),
            P(),
            P(),
        ),
        out_specs=(P("chaos", "gx", "gy", None), P("chaos", "gx", "gy", None)),
        check_vma=False,
    )
```
